32 devices in a mesh: space: 4 (over y, core), mode: 8 (over z, x).
Axes of the slice: x: 2, y: 2, z: 4, core: 2. Of those that a mesh axis runs over, the one named last changes fastest.
Arguments:
- intensity: float32 [1024, 8, 64, 256], P('mode', None, 'space'), may hold values from 0.1 to 2
- dir_cos: float32 [3, 32], replicated, may hold values from -1 to 1, as said below
- velocity: float32 [32], replicated, may hold values from 0.2 to 1
- rate: float32 [32], replicated, may hold values from 0.05 to 2
- spectrum: float32 [32], replicated, may hold values from 0.2 to 2
- weight: float32 [32], replicated, may hold values from 0.25 to 1.75
- heat: float32 [64, 256], P('space'), may hold values from 0.5 to 4
- rough_cells: int32 [4096], P('space'), may hold values from 0 to 4095, as said below
- rough_count: int32 [4], P('space'), may hold values from 256 to 1024, as said below
- rough_map: int32 [4096, 16], P('space'), may hold values from 0 to 15
Outputs:
- intensity_new: float32 [1024, 8, 64, 256], P('mode', None, 'space')
- energy_new: float32 [8, 64, 256], P(None, 'space')
The draws below stay inside these ranges and needn't reach their ends.
Inputs may be any that keep to these rules, and one draw needn't show every extreme that they name: `dir_cos`: even directions have a positive third cosine, and direction 2k+1 equals direction 2k with the third cosine negated; every direction has a third cosine of magnitude 0.3 or more. `rough_cells`: the entries of one index of space are distinct. `rough_count`: some index of space has all 1024 slots live.
All inputs are finite; a program needn't handle non-finite values.
Results may differ from the reference program's by a relative error of at most 0.0015.
Values sent between devices are 32-bit elements; how exact they have to be, the bound alone decides.
A program may use at most 128 MiB of HBM per device.

```python
import math
import jax
import jax.numpy as jnp

DIRS = 32
MODES = 32
Z = 8
XR = 16
NY = 256
PAIRS = 1024
NX = 64
ROUGH = 1024
N_SPACE = 4


def draw_dir_cos(key, part):
    keys = jax.random.split(jax.random.fold_in(key, 11), 3)
    half = DIRS // 2
    ux = jax.random.normal(keys[0], (half,), jnp.float32)
    uy = jax.random.normal(keys[1], (half,), jnp.float32)
    uz = jax.random.uniform(keys[2], (half,), jnp.float32, 0.6, 1.6)
    length = jnp.sqrt(ux * ux + uy * uy + uz * uz)
    ux = ux / length
    uy = uy / length
    uz = jnp.maximum(uz / length, 0.3)
    cx = jnp.stack([ux, ux], axis=1).reshape(DIRS)
    cy = jnp.stack([uy, uy], axis=1).reshape(DIRS)
    cz = jnp.stack([uz, -uz], axis=1).reshape(DIRS)
    return jnp.stack([cx, cy, cz], axis=0).astype(jnp.float32)


def draw_rough_cells(key, part):
    keys = jax.random.split(jax.random.fold_in(key, 23), N_SPACE)
    lists = jax.vmap(lambda k: jax.random.permutation(k, XR * NY)[:ROUGH])(keys)
    return lists.reshape(-1).astype(jnp.int32)


def draw_rough_count(key, part):
    keys = jax.random.split(jax.random.fold_in(key, 37), 2)
    counts = jax.random.randint(keys[0], (N_SPACE,), ROUGH // 4, ROUGH + 1)
    fullest = jax.random.randint(keys[1], (), 0, N_SPACE)
    return counts.at[fullest].set(ROUGH).astype(jnp.int32)


def touch_ends(array, rng, smallest, top_value):
    spot = [jax.random.randint(jax.random.fold_in(rng, axis), (), 0, length) for axis, length in enumerate(array.shape)]
    main_axis = array.shape.index(max(array.shape))
    neighbour = spot[:main_axis] + [(spot[main_axis] + 1) % array.shape[main_axis]] + spot[main_axis + 1:]
    return array.at[tuple(spot)].set(smallest).at[tuple(neighbour)].set(top_value)


def block_levels(key, shape, cuts, least, largest):
    def one(position, parts):
        draws = jax.random.uniform(jax.random.fold_in(jax.random.fold_in(key, 6), position), (parts,), jnp.float32, least / len(cuts), largest / len(cuts))
        return jnp.repeat(jnp.exp(draws), shape[position] // parts).reshape((-1,) + (1,) * (len(shape) - position - 1))

    loudness = one(*cuts[0])
    for cut in cuts[1:]:
        loudness = loudness * one(*cut)
    return loudness


def setup_inputs(seed: int = 0) -> dict:
    seeds = jax.random.split(jax.random.key(seed), 11)
    return {
        "intensity": jnp.clip(jnp.exp(math.log(2.0) - 2.9957323 * jax.random.uniform(seeds[0], (PAIRS, Z, NX, NY), jnp.float32) ** block_levels(seeds[0], (PAIRS, Z, NX, NY), ((0, 8), (2, 4)), -0.2, 0.2)), 0.1, 2.0),
        "dir_cos": draw_dir_cos(jax.random.fold_in(seeds[10], 71), 0),
        "velocity": jnp.clip(jnp.exp(jax.random.uniform(seeds[2], (MODES,), jnp.float32, math.log(0.2), math.log(1.0))), 0.2, 1.0),
        "rate": jnp.clip(jnp.exp(jax.random.uniform(seeds[3], (MODES,), jnp.float32, math.log(0.05), math.log(2.0))), 0.05, 2.0),
        "spectrum": jnp.clip(jnp.exp(jax.random.uniform(seeds[4], (MODES,), jnp.float32, math.log(0.2), math.log(2.0))), 0.2, 2.0),
        "weight": jnp.clip(1.0 + 0.15 * jax.random.normal(seeds[5], (DIRS,), jnp.float32), 0.25, 1.75),
        "heat": jnp.clip(jnp.exp(math.log(4.0) - 2.0794415 * jax.random.uniform(seeds[6], (NX, NY), jnp.float32) ** block_levels(seeds[6], (NX, NY), ((0, 4),), -0.2, 0.2)), 0.5, 4.0),
        "rough_cells": draw_rough_cells(jax.random.fold_in(seeds[10], 71), 0),
        "rough_count": draw_rough_count(jax.random.fold_in(seeds[10], 71), 0),
        "rough_map": touch_ends(jax.random.randint(seeds[9], (N_SPACE * ROUGH, DIRS // 2), 0, DIRS // 2), jax.random.fold_in(seeds[9], 1), 0, (DIRS // 2) - 1).astype(jnp.int32),
    }


def drift_of(field, dir_cos, velocity):
    ox = dir_cos[0][:, None, None, None, None]
    oy = dir_cos[1][:, None, None, None, None]
    speed = velocity[None, :, None, None, None]
    padx = jnp.pad(field, ((0, 0), (0, 0), (0, 0), (1, 1), (0, 0)))
    pady = jnp.pad(field, ((0, 0), (0, 0), (0, 0), (0, 0), (1, 1)))
    along = jnp.maximum(ox, 0.0) * (field - padx[:, :, :, :-2]) + jnp.minimum(ox, 0.0) * (padx[:, :, :, 2:] - field)
    across = jnp.maximum(oy, 0.0) * (field - pady[..., :-2]) + jnp.minimum(oy, 0.0) * (pady[..., 2:] - field)
    return speed * (along + across)


def reference(intensity, dir_cos, velocity, rate, spectrum, weight, heat, rough_cells, rough_count, rough_map):
    field = intensity.reshape(DIRS, MODES, Z, NX, NY)
    energy = jnp.einsum('s,smzxy->zxy', weight, field) / PAIRS
    equil = energy / (1.0 + 0.3 * jnp.abs(energy))
    source = (rate * spectrum)[:, None, None, None] * equil[None]
    rhs = field + source[None] - drift_of(field, dir_cos, velocity)
    diag = 1.0 + rate
    couple = velocity[None, :] * jnp.abs(dir_cos[2])[:, None]
    up_rhs = rhs[0::2]
    down_rhs = rhs[1::2]
    cdown = couple[1::2][:, :, None, None]
    adown = diag[None, :, None, None] + cdown
    carry = spectrum[None, :, None, None] * heat[None, None]
    planes = [None] * Z
    for level in reversed(range(Z)):
        carry = (down_rhs[:, :, level] + cdown * carry) / adown
        planes[level] = carry
    down_new = jnp.stack(planes, axis=2)
    bottom = down_new[:, :, 0].reshape(DIRS // 2, MODES, NX * NY)
    offsets = jnp.arange(N_SPACE, dtype=jnp.int32) * (XR * NY)
    cells = (rough_cells.reshape(N_SPACE, ROUGH) + offsets[:, None]).reshape(-1).astype(jnp.int32)
    live = (jnp.arange(ROUGH, dtype=jnp.int32)[None, :] < rough_count[:, None]).reshape(-1)
    values = bottom[:, :, cells].transpose(2, 0, 1)
    picked = jnp.take_along_axis(values, rough_map[:, :, None], axis=1).transpose(1, 2, 0)
    current = bottom[:, :, cells]
    inflow = 0.9 * bottom.at[:, :, cells].set(jnp.where(live[None, None, :], picked, current))
    inflow = inflow.reshape(DIRS // 2, MODES, NX, NY)
    cup = couple[0::2][:, :, None, None]
    aup = diag[None, :, None, None] + cup
    carry = inflow
    planes = []
    for level in range(Z):
        carry = (up_rhs[:, :, level] + cup * carry) / aup
        planes.append(carry)
    up_new = jnp.stack(planes, axis=2)
    fresh = jnp.stack([up_new, down_new], axis=1).reshape(DIRS, MODES, Z, NX, NY)
    energy_new = jnp.einsum('s,smzxy->zxy', weight, fresh) / PAIRS
    return fresh.reshape(PAIRS, Z, NX, NY), energy_new
```

```python
import functools

import jax
import jax.numpy as jnp
from jax import lax
from jax.experimental import pallas as pl
from jax.experimental.pallas import tpu as pltpu
from jax.sharding import PartitionSpec as P

MESH = pl.DeviceIdType.MESH
F32 = jnp.float32
BF16 = jnp.bfloat16
SUB, LANE = 8, 128
MIB = 1 << 20


def whole(space=pltpu.VMEM):
    return pl.BlockSpec(memory_space=space)


def squash(energy):
    return energy / (1.0 + 0.3 * jnp.abs(energy))


def send(src, dst, ssem, rsem, axis, target):
    return pltpu.make_async_remote_copy(
        src_ref=src,
        dst_ref=dst,
        send_sem=ssem,
        recv_sem=rsem,
        device_id={axis: target},
        device_id_type=MESH,
    )


class Reduction:
    def __init__(self, acc, slots, part, total, sems, n):
        self.acc, self.slots, self.part, self.total = acc, slots, part, total
        self.sems, self.n = sems, n
        self.me = lax.axis_index("mode")
        self.rows = acc.shape[0] // n

    def chunk(self, i):
        return pl.ds(pl.multiple_of(i * self.rows, self.rows), self.rows)

    def outward(self, off):
        target = lax.rem(self.me + off, self.n)
        return send(
            self.acc.at[self.chunk(target)], self.slots.at[off],
            self.sems.at[0, off], self.sems.at[1, off], "mode", target,
        )

    def spread(self, off):
        target = lax.rem(self.me + off, self.n)
        return send(
            self.part, self.total.at[self.chunk(self.me)],
            self.sems.at[2, off], self.sems.at[3, off], "mode", target,
        )

    def start(self):
        for off in range(1, self.n):
            self.outward(off).start()

    def combine(self, finish):
        for off in range(1, self.n):
            self.outward(off).wait_recv()
        value = self.acc[self.chunk(self.me), :]
        for off in range(1, self.n):
            value = value + self.slots[off]
        self.part[...] = finish(value)
        for off in range(1, self.n):
            self.spread(off).start()
        self.total[self.chunk(self.me), :] = self.part[...]

    def finish(self):
        for off in range(1, self.n):
            source = lax.rem(self.me + self.n - off, self.n)
            send(
                self.part, self.total.at[self.chunk(source)],
                self.sems.at[2, off], self.sems.at[3, off], "mode", source,
            ).wait_recv()
        for off in range(1, self.n):
            self.outward(off).wait_send()
            self.spread(off).wait_send()


def split(value):
    high = value.astype(BF16)
    return high, (value - high.astype(F32)).astype(BF16)


def splat(value):
    return jnp.full((SUB, LANE), value, F32)


def tiles(rows, width):
    return [(r, c) for r in range(0, rows, SUB) for c in range(0, width, LANE)]


def main_kernel(
    n, ns, planes,
    count, dir_cos, velocity, rate, spectrum, weight, heat, cells, reflect, x,
    xv, inflow, energy,
    lo, hi, first, last, acc, slots1, part1, equil, acc2, slots2, part2,
    held, picked, marks, lsem, hsem, sems1, sems2, ssem, rsem,
):
    me, sp = lax.axis_index("mode"), lax.axis_index("space")
    pairs, total_rows, width = xv.shape
    rows = total_rows // planes
    modes = velocity.shape[0]
    dirs = pairs // modes
    half = dirs // 2
    quiet = half * modes
    pairs_total = pairs * n
    rough = cells.shape[1]
    batch = min(16, modes)
    per_dir = modes // batch
    order = [d for d in range(1, dirs, 2)] + [d for d in range(0, dirs, 2)]
    chunks = [(d, b) for d in order for b in range(per_dir)]

    def load(i):
        d, b = chunks[i]
        where = pl.ds(d * modes + b * batch, batch)
        return pltpu.make_async_copy(x.at[where], xv.at[where], lsem.at[i])

    for i in range(len(chunks)):
        load(i).start()

    def place_of(index):
        return jnp.where(lax.rem(index, 2) == 0, index // 2, n - 1 - index // 2)

    def index_of(place):
        place = lax.rem(place + n, n)
        return jnp.where(place < n // 2, 2 * place, 2 * (n - 1 - place) + 1)

    place = place_of(me)
    ends = (index_of(place + 1), index_of(place - 1))

    barrier = pltpu.get_barrier_semaphore()
    for off in range(1, n):
        pl.semaphore_signal(
            barrier, inc=1, device_id={"mode": lax.rem(me + off, n)}, device_id_type=MESH
        )

    @pl.when(sp > 0)
    def _():
        pl.semaphore_signal(barrier, inc=1, device_id={"space": sp - 1}, device_id_type=MESH)

    @pl.when(sp < ns - 1)
    def _():
        pl.semaphore_signal(barrier, inc=1, device_id={"space": sp + 1}, device_id_type=MESH)

    @pl.when(sp == 0)
    def _():
        lo[...] = jnp.zeros_like(lo)

    @pl.when(sp == ns - 1)
    def _():
        hi[...] = jnp.zeros_like(hi)

    acc[...] = jnp.zeros_like(acc)
    acc2[...] = jnp.zeros_like(acc2)
    marks[...] = jnp.where(
        lax.broadcasted_iota(jnp.int32, (width, rough), 0) == lax.rem(cells[...], width), 1.0, 0.0
    ).astype(BF16)

    low = jnp.where(sp > 0, 1, 0)
    high = jnp.where(sp < ns - 1, 1, 0)
    pl.semaphore_wait(barrier, n - 1 + low + high)

    def down_copy(i):
        d, b = chunks[i]
        where = pl.ds(d * modes + b * batch, batch)
        return send(
            first.at[where], hi.at[where], hsem.at[0, i], hsem.at[1, i], "space",
            lax.rem(sp + ns - 1, ns),
        )

    def up_copy(i):
        d, b = chunks[i]
        where = pl.ds(d * modes + b * batch, batch)
        return send(
            last.at[where], lo.at[where], hsem.at[2, i], hsem.at[3, i], "space",
            lax.rem(sp + 1, ns),
        )

    for i, (d, b) in enumerate(chunks):
        base = d * modes + b * batch
        load(i).wait()

        def edges(t, carry):
            p = base + t
            for z in range(planes):
                first[p, pl.ds(z, 1), :] = xv[p, pl.ds(z * rows, 1), :]
                last[p, pl.ds(z, 1), :] = xv[p, pl.ds((z + 1) * rows - 1, 1), :]
            return carry

        lax.fori_loop(0, batch, edges, 0)

        @pl.when(sp > 0)
        def _():
            down_copy(i).start()

        @pl.when(sp < ns - 1)
        def _():
            up_copy(i).start()

        w = weight[me * dirs + d]

        def add_rows(r, carry):
            here = pl.ds(pl.multiple_of(r * SUB, SUB), SUB)
            value = xv[base, here, :]
            for t in range(1, batch):
                value = value + xv[base + t, here, :]
            acc[here, :] += w * value
            return carry

        lax.fori_loop(0, total_rows // SUB, add_rows, 0)

    opening = Reduction(acc, slots1, part1, equil, sems1, n)
    opening.start()

    row = lax.broadcasted_iota(jnp.int32, (SUB, LANE), 0)
    lane = lax.broadcasted_iota(jnp.int32, (SUB, LANE), 1)
    places = tiles(rows, width)
    last_row, last_col = rows - SUB, width - LANE

    def factors(d, m):
        s = me * dirs + d
        v = velocity[m]
        turn = v * jnp.abs(dir_cos[2, s])
        inv = 1.0 / splat(1.0 + rate[m] + turn)
        return v * jnp.abs(dir_cos[0, s]), v * jnp.abs(dir_cos[1, s]), turn, inv

    def sweep(d, start, stop):
        s = me * dirs + d
        low_x, low_y = splat(dir_cos[0, s]) >= 0.0, splat(dir_cos[1, s]) >= 0.0
        shift_x = jnp.where(dir_cos[0, s] >= 0.0, 1, SUB - 1)
        shift_y = jnp.where(dir_cos[1, s] >= 0.0, 1, LANE - 1)
        wrap_x = (low_x & (row == 0)) | (~low_x & (row == SUB - 1))
        wrap_y = (low_y & (lane == 0)) | (~low_y & (lane == LANE - 1))
        wide = 2

        def some(g, carry):
            sets = []
            for t in range(wide):
                m = start + g * wide + t
                vx, vy, turn, inv = factors(d, m)
                kx, ky = inv * vx, inv * vy
                sets.append((
                    d * modes + m, inv * (1.0 - vx - vy), kx, ky, inv * turn,
                    jnp.where(low_x & (row == 0), 0.0, kx),
                    jnp.where(~low_x & (row == SUB - 1), 0.0, kx),
                    jnp.where(low_y & (lane == 0), 0.0, ky),
                    jnp.where(~low_y & (lane == LANE - 1), 0.0, ky),
                ))
            before = [None] * wide
            for z in range(planes) if d % 2 == 0 else reversed(range(planes)):
                for t in range(wide):
                    p, k0, kx, ky, kp, kx_top, kx_end, ky_top, ky_end = sets[t]
                    own = {
                        (r, c): xv[p, pl.ds(z * rows + r, SUB), pl.ds(c, LANE)] for r, c in places
                    }
                    side = {at: pltpu.roll(own[at], shift_x, 0) for at in places}
                    along = {at: pltpu.roll(own[at], shift_y, 1) for at in places}
                    now = {}
                    for r, c in places:
                        one = side[r, c]
                        if rows > SUB:
                            below = side[(r - SUB) % rows, c]
                            above = side[(r + SUB) % rows, c]
                            one = jnp.where(wrap_x, jnp.where(low_x, below, above), one)
                        two = along[r, c]
                        if width > LANE:
                            left = along[r, (c - LANE) % width]
                            right = along[r, (c + LANE) % width]
                            two = jnp.where(wrap_y, jnp.where(low_y, left, right), two)
                        gain_x = kx
                        if r == 0:
                            gain_x = kx_top
                        if r == last_row:
                            gain_x = kx_end if r else jnp.where(wrap_x, 0.0, kx)
                        gain_y = ky
                        if c == 0:
                            gain_y = ky_top
                        if c == last_col:
                            gain_y = ky_end if c else jnp.where(wrap_y, 0.0, ky)
                        value = k0 * own[r, c] + gain_x * one + gain_y * two
                        if before[t] is not None:
                            value = value + kp * before[t][r, c]
                        now[r, c] = value
                        xv[p, pl.ds(z * rows + r, SUB), pl.ds(c, LANE)] = value
                    before[t] = now
            return carry

        lax.fori_loop(0, (stop - start) // wide, some, 0)

    def settle(d, start, stop):
        s = me * dirs + d
        low_x = splat(dir_cos[0, s]) >= 0.0
        w = weight[s]
        wide = min(4, stop - start)

        def some(g, carry):
            sets = []
            for t in range(wide):
                m = start + g * wide + t
                vx, _, turn, inv = factors(d, m)
                kx = inv * vx
                sets.append((
                    d * modes + m, inv * turn, inv * (rate[m] * spectrum[m]),
                    jnp.where(low_x & (row == 0), kx, 0.0),
                    jnp.where(~low_x & (row == SUB - 1), kx, 0.0),
                ))
            values = []
            for t in range(wide):
                m = start + g * wide + t
                values.append({
                    (r, c): heat[pl.ds(r, SUB), pl.ds(c, LANE)] * spectrum[m] if d % 2 else None
                    for r, c in places
                })
            for z in range(planes) if d % 2 == 0 else reversed(range(planes)):
                for r, c in places:
                    here, cols = pl.ds(z * rows + r, SUB), pl.ds(c, LANE)
                    level = equil[here, cols]
                    total = None
                    for t in range(wide):
                        p, kp, ks, k_low, k_high = sets[t]
                        value = ks * level
                        if values[t][r, c] is not None:
                            value = value + kp * values[t][r, c]
                        if r == 0:
                            edge = lo[p, pl.ds(z, 1), cols]
                            value = value + k_low * jnp.broadcast_to(edge, (SUB, LANE))
                        if r == last_row:
                            edge = hi[p, pl.ds(z, 1), cols]
                            value = value + k_high * jnp.broadcast_to(edge, (SUB, LANE))
                        values[t][r, c] = value
                        out = xv[p, here, cols] + value
                        xv[p, here, cols] = out
                        total = out if total is None else total + out
                    acc2[here, cols] += w * total
            return carry

        lax.fori_loop(0, (stop - start) // wide, some, 0)

    def halo_wait(i):
        @pl.when(sp > 0)
        def _():
            down_copy(i).wait_send()
            up_copy(i).wait_recv()

        @pl.when(sp < ns - 1)
        def _():
            up_copy(i).wait_send()
            down_copy(i).wait_recv()

    for d in range(1, dirs, 2):
        sweep(d, 0, modes)
    opening.combine(lambda value: squash(value * (1.0 / pairs_total)))
    for d in range(0, dirs, 2):
        sweep(d, 0, modes)
    opening.finish()

    row_of = cells[...] // width
    on_row = jnp.where(lax.broadcasted_iota(jnp.int32, (rows, rough), 0) == row_of, 1.0, 0.0)
    piece = quiet // 4

    def rows_of(way, part):
        return (2 * way + part) * piece

    def pair_of(q):
        return (2 * (q // modes) + 1) * modes + q % modes

    def gather(q):
        bottom = xv[pl.ds(pair_of(q), piece), pl.ds(0, rows), :]
        high, low = split(bottom.reshape(piece * rows, width))
        column = marks[...]
        got = jnp.dot(high, column, preferred_element_type=F32) + jnp.dot(
            low, column, preferred_element_type=F32
        )
        held[place, pl.ds(q, piece), :] = jnp.sum(
            got.reshape(piece, rows, rough) * on_row[None], axis=1
        )

    def slot_of(way, step):
        return lax.rem(place + n + (-step if way == 0 else step), n)

    def copy_of(way, part, step):
        at = held.at[slot_of(way, step), pl.ds(rows_of(way, part), piece)]
        return send(at, at, ssem.at[way, part, step], rsem.at[way, part, step], "mode", ends[way])

    def arrival(way, part, step):
        at = held.at[slot_of(way, step + 1), pl.ds(rows_of(way, part), piece)]
        return send(at, at, ssem.at[way, part, step], rsem.at[way, part, step], "mode", ends[way])

    def choose(way, step):
        slot = slot_of(way, step)
        owner = index_of(slot)
        for h in range(half):
            want = reflect[pl.ds(me * half + h, 1), :]
            for q in range(rows_of(way, 0), rows_of(way, 0) + 2 * piece, SUB):
                j, m = q // modes, q % modes
                here = pl.ds(h * modes + m, SUB)
                picked[here, :] = jnp.where(
                    want == owner * half + j, held[slot, pl.ds(q, SUB), :], picked[here, :]
                )

    picked[...] = jnp.zeros_like(picked)
    waited = set()
    for part in range(2):
        for way in range(2):
            q = rows_of(way, part)
            d, m = 2 * (q // modes) + 1, q % modes
            for i, (dd, b) in enumerate(chunks):
                if dd == d and b * batch < m + piece and m < (b + 1) * batch and i not in waited:
                    waited.add(i)
                    halo_wait(i)
            settle(d, m, m + piece)
            gather(q)
            copy_of(way, part, 0).start()
    for i in range(len(chunks)):
        if i not in waited:
            halo_wait(i)
    for way in range(2):
        choose(way, 0)

    tasks = [(d, m) for d in range(0, dirs, 2) for m in range(0, modes, SUB)]
    per_step = -(-len(tasks) // (n - 2))
    for step in range(1, n):
        for part in range(2):
            for way in range(2):
                arrival(way, part, step - 1).wait_recv()
                if step < n - 1:
                    copy_of(way, part, step).start()
        for way in range(2):
            choose(way, step)
        for d, m in tasks[(step - 1) * per_step : step * per_step]:
            settle(d, m, m + SUB)
    for step in range(n - 1):
        for part in range(2):
            for way in range(2):
                copy_of(way, part, step).wait_send()

    live = jnp.where(lax.broadcasted_iota(jnp.int32, (rows, rough), 1) < count[0], on_row, 0.0)
    contract = (((1,), (1,)), ((), ()))
    is_rough = lax.dot_general(live.astype(BF16), marks[...], contract, preferred_element_type=F32)
    is_rough = (is_rough > 0.5)[None]

    def scatter(g, carry):
        q = pl.multiple_of(g * piece, piece)
        spread = (picked[pl.ds(q, piece), :][:, None, :] * live[None]).reshape(piece * rows, rough)
        high, low = split(spread)
        column = marks[...]
        put = lax.dot_general(
            high, column, contract, preferred_element_type=F32
        ) + lax.dot_general(low, column, contract, preferred_element_type=F32)
        bottom = xv[pl.ds(pair_of(q), piece), pl.ds(0, rows), :]
        inflow[pl.ds(q, piece)] = 0.9 * jnp.where(
            is_rough, put.reshape(piece, rows, width), bottom
        )
        return carry

    lax.fori_loop(0, quiet // piece, scatter, 0)

    def rise(h):
        d = 2 * h
        w = weight[me * dirs + d]
        wide = 4

        def some(g, carry):
            sets, values = [], []
            for t in range(wide):
                m = g * wide + t
                _, _, turn, inv = factors(d, m)
                sets.append(inv * turn)
                values.append({
                    (r, c): inflow[h * modes + m, pl.ds(r, SUB), pl.ds(c, LANE)] for r, c in places
                })
            for z in range(planes):
                for r, c in places:
                    here, cols = pl.ds(z * rows + r, SUB), pl.ds(c, LANE)
                    total = None
                    for t in range(wide):
                        value = sets[t] * values[t][r, c]
                        values[t][r, c] = value
                        total = value if total is None else total + value
                    acc2[here, cols] += w * total
            return carry

        lax.fori_loop(0, modes // wide, some, 0)

    for h in range(half):
        rise(h)
    closing = Reduction(acc2, slots2, part2, energy, sems2, n)
    closing.start()
    closing.combine(lambda value: value * (1.0 / pairs_total))
    closing.finish()


def main_step(scalars, count, heat, cells, reflect, x, n, ns, planes):
    pairs, total_rows, width = x.shape
    rows = total_rows // planes
    modes = scalars[1].shape[0]
    quiet = pairs // 2
    rough = cells.shape[1]
    n_chunks = (pairs // modes) * (modes // min(16, modes))
    flat = (total_rows, width)
    part = (total_rows // n, width)
    halo = pltpu.VMEM((pairs, planes, width), F32)
    return pl.pallas_call(
        functools.partial(main_kernel, n, ns, planes),
        out_shape=(
            jax.ShapeDtypeStruct(x.shape, F32),
            jax.ShapeDtypeStruct((quiet, rows, width), F32),
            jax.ShapeDtypeStruct(flat, F32),
        ),
        in_specs=[whole(pltpu.SMEM)] * 6 + [whole()] * 3 + [whole(pltpu.HBM)],
        out_specs=(whole(),) * 3,
        scratch_shapes=[
            halo, halo, halo, halo,
            pltpu.VMEM(flat, F32),
            pltpu.VMEM((n, *part), F32),
            pltpu.VMEM(part, F32),
            pltpu.VMEM(flat, F32),
            pltpu.VMEM(flat, F32),
            pltpu.VMEM((n, *part), F32),
            pltpu.VMEM(part, F32),
            pltpu.VMEM((n, quiet, rough), F32),
            pltpu.VMEM((quiet, rough), F32),
            pltpu.VMEM((width, rough), BF16),
            pltpu.SemaphoreType.DMA((n_chunks,)),
            pltpu.SemaphoreType.DMA((4, n_chunks)),
            pltpu.SemaphoreType.DMA((4, n)),
            pltpu.SemaphoreType.DMA((4, n)),
            pltpu.SemaphoreType.DMA((2, 2, n - 1)),
            pltpu.SemaphoreType.DMA((2, 2, n - 1)),
        ],
        compiler_params=pltpu.CompilerParams(
            collective_id=0, has_side_effects=True, vmem_limit_bytes=30 * MIB
        ),
        name="main_step",
    )(count, *scalars, heat, cells, reflect, x)


def emit_kernel(
    planes, dir_cos, velocity, rate, xv, inflow, summed, out, energy, rising, sem
):
    pairs, total_rows, width = xv.shape
    rows = total_rows // planes
    modes = velocity.shape[0]
    dirs = pairs // modes
    batch = min(8, modes)
    me = lax.axis_index("mode")
    places = tiles(rows, width)

    def whole_dir(d):
        where = pl.ds(d * modes, modes)
        return pltpu.make_async_copy(xv.at[where], out.at[where], sem.at[d, 0])

    def piece(d, b):
        return pltpu.make_async_copy(
            rising.at[pl.ds(d // 2 * modes + b * batch, batch)],
            out.at[pl.ds(d * modes + b * batch, batch)], sem.at[d, b],
        )

    for d in range(1, dirs, 2):
        whole_dir(d).start()
    energy[...] = summed[...]
    for d in range(0, dirs, 2):
        cz = jnp.abs(dir_cos[2, me * dirs + d])
        for b in range(modes // batch):
            def one(i, carry):
                m = b * batch + i
                turn = velocity[m] * cz
                ratio = splat(turn) / splat(1.0 + rate[m] + turn)
                q = d // 2 * modes + m
                for r, c in places:
                    cols = pl.ds(c, LANE)
                    value = inflow[q, pl.ds(r, SUB), cols]
                    for z in range(planes):
                        here = pl.ds(z * rows + r, SUB)
                        value = ratio * value
                        rising[q, here, cols] = xv[d * modes + m, here, cols] + value
                return carry

            lax.fori_loop(0, batch, one, 0)
            piece(d, b).start()
    for d in range(dirs):
        if d % 2:
            whole_dir(d).wait()
        else:
            for b in range(modes // batch):
                piece(d, b).wait()


def emit_step(planes, scalars, xv, inflow, summed):
    pairs, total_rows, width = xv.shape
    modes = scalars[1].shape[0]
    return pl.pallas_call(
        functools.partial(emit_kernel, planes),
        out_shape=(
            jax.ShapeDtypeStruct(xv.shape, F32),
            jax.ShapeDtypeStruct(summed.shape, F32),
        ),
        in_specs=[whole(pltpu.SMEM)] * 3 + [whole()] * 3,
        out_specs=(whole(pltpu.HBM), whole()),
        scratch_shapes=[
            pltpu.VMEM((pairs // 2, total_rows, width), F32),
            pltpu.SemaphoreType.DMA((pairs // modes, modes // min(8, modes))),
        ],
        compiler_params=pltpu.CompilerParams(vmem_limit_bytes=16 * MIB),
        name="emit_step",
    )(*scalars[:3], xv, inflow, summed)


def per_device(
    n, ns, intensity, dir_cos, velocity, rate, spectrum, weight, heat, rough_cells, rough_count,
    rough_map,
):
    pairs, planes, rows, width = intensity.shape
    x = intensity.reshape(pairs, planes * rows, width)
    scalars = (dir_cos, velocity, rate, spectrum, weight)
    xv, inflow, summed = main_step(
        scalars, rough_count, heat, rough_cells[None], rough_map.T, x, n, ns, planes
    )
    fresh, energy = emit_step(planes, scalars, xv, inflow, summed)
    return fresh.reshape(intensity.shape), energy.reshape(planes, rows, width)


def solution(mesh):
    n, ns = mesh.shape["mode"], mesh.shape["space"]
    in_specs = (
        P("mode", None, "space", None),
        P(),
        P(),
        P(),
        P(),
        P(),
        P("space", None),
        P("space"),
        P("space"),
        P("space", None),
    )
    out_specs = (P("mode", None, "space", None), P(None, "space", None))
    return jax.shard_map(
        functools.partial(per_device, n, ns),
        mesh=mesh,
        in_specs=in_specs,
        out_specs=out_specs,
        check_vma=False,
    )
```

```python
import functools

import jax
import jax.numpy as jnp
from jax import lax
from jax.experimental import pallas as pl
from jax.experimental.pallas import tpu as pltpu
from jax.sharding import PartitionSpec as P

MESH = pl.DeviceIdType.MESH
F32 = jnp.float32
BF16 = jnp.bfloat16
SUB, LANE = 8, 128
MIB = 1 << 20


def whole(space=pltpu.VMEM):
    return pl.BlockSpec(memory_space=space)


def in_hbm(*arrays):
    return tuple(pltpu.with_memory_space_constraint(a, pltpu.HBM) for a in arrays)


def squash(energy):
    return energy / (1.0 + 0.3 * jnp.abs(energy))


def send(src, dst, ssem, rsem, axis, target):
    return pltpu.make_async_remote_copy(
        src_ref=src,
        dst_ref=dst,
        send_sem=ssem,
        recv_sem=rsem,
        device_id={axis: target},
        device_id_type=MESH,
    )


class Reduction:
    def __init__(self, acc, slots, part, total, sems, n):
        self.acc, self.slots, self.part, self.total = acc, slots, part, total
        self.sems, self.n = sems, n
        self.me = lax.axis_index("mode")
        self.rows = acc.shape[0] // n

    def chunk(self, i):
        return pl.ds(pl.multiple_of(i * self.rows, self.rows), self.rows)

    def outward(self, off):
        target = lax.rem(self.me + off, self.n)
        return send(
            self.acc.at[self.chunk(target)], self.slots.at[off],
            self.sems.at[0, off], self.sems.at[1, off], "mode", target,
        )

    def spread(self, off):
        target = lax.rem(self.me + off, self.n)
        return send(
            self.part, self.total.at[self.chunk(self.me)],
            self.sems.at[2, off], self.sems.at[3, off], "mode", target,
        )

    def start(self):
        for off in range(1, self.n):
            self.outward(off).start()

    def combine(self, finish):
        for off in range(1, self.n):
            self.outward(off).wait_recv()
        value = self.acc[self.chunk(self.me), :]
        for off in range(1, self.n):
            value = value + self.slots[off]
        self.part[...] = finish(value)
        for off in range(1, self.n):
            self.spread(off).start()
        self.total[self.chunk(self.me), :] = self.part[...]

    def finish(self):
        for off in range(1, self.n):
            source = lax.rem(self.me + self.n - off, self.n)
            send(
                self.part, self.total.at[self.chunk(source)],
                self.sems.at[2, off], self.sems.at[3, off], "mode", source,
            ).wait_recv()
        for off in range(1, self.n):
            self.outward(off).wait_send()
            self.spread(off).wait_send()


def split(value):
    high = value.astype(BF16)
    return high, (value - high.astype(F32)).astype(BF16)


def splat(value):
    return jnp.full((SUB, LANE), value, F32)


def tiles(rows, width):
    return [(r, c) for r in range(0, rows, SUB) for c in range(0, width, LANE)]


def dot(a, b):
    return jnp.dot(a, b, preferred_element_type=F32)


def fine_dot(a, b):
    a_high, a_low = split(a)
    b_high, b_low = split(b)
    return dot(a_high, b_high) + (dot(a_high, b_low) + dot(a_low, b_high))


def turned_dot(a, b):
    contract = (((1,), (1,)), ((), ()))
    high, low = split(a)
    return lax.dot_general(high, b, contract, preferred_element_type=F32) + lax.dot_general(
        low, b, contract, preferred_element_type=F32
    )


def iota(shape, axis):
    return lax.broadcasted_iota(jnp.int32, shape, axis)


def copies(pairs, sem):
    return [pltpu.make_async_copy(src, dst, sem.at[i]) for i, (src, dst) in enumerate(pairs)]


def main_kernel(
    n, ns, planes,
    count, dir_cos_in, velocity_in, rate_in, spectrum_in, weight_in, heat_in, cells_in, reflect_in,
    x,
    xv, picked, equil, summed, smooth, live, marks,
    dir_cos, velocity, rate, spectrum, weight, dir_row, velocity_row, rate_row, spectrum_row,
    heat, cells, reflect,
    lo, hi, first, last, acc, slots1, part1, acc2, slots2, part2,
    held, block, lift, on_row, response, psem, lsem, hsem, sems1, sems2, ssem, rsem,
):
    me, sp = lax.axis_index("mode"), lax.axis_index("space")
    pairs, total_rows, width = xv.shape
    rows = total_rows // planes
    modes = velocity.shape[1]
    dirs = pairs // modes
    half = dirs // 2
    quiet = half * modes
    ups = reflect.shape[0]
    pairs_total = pairs * n
    rough = cells.shape[1]
    piece = quiet // 4
    batch = min(16, modes)
    per_dir = modes // batch
    order = [d for d in range(1, dirs, 2)] + [d for d in range(0, dirs, 2)]
    chunks = [(d, b) for d in order for b in range(per_dir)]

    fetched = copies((
        (cells_in, cells), (weight_in, weight), (dir_cos_in, dir_cos), (velocity_in, velocity),
        (rate_in, rate), (spectrum_in, spectrum), (dir_cos_in, dir_row),
        (velocity_in, velocity_row), (rate_in, rate_row), (spectrum_in, spectrum_row),
        (heat_in, heat), (reflect_in, reflect),
    ), psem)
    for copy in fetched:
        copy.start()

    def load(i):
        d, b = chunks[i]
        where = pl.ds(d * modes + b * batch, batch)
        return pltpu.make_async_copy(x.at[where], xv.at[where], lsem.at[i])

    for i in range(len(chunks)):
        load(i).start()

    def place_of(index):
        return jnp.where(lax.rem(index, 2) == 0, index // 2, n - 1 - index // 2)

    def index_of(place):
        place = lax.rem(place + n, n)
        return jnp.where(place < n // 2, 2 * place, 2 * (n - 1 - place) + 1)

    place = place_of(me)
    ends = (index_of(place + 1), index_of(place - 1))

    barrier = pltpu.get_barrier_semaphore()
    for off in range(1, n):
        pl.semaphore_signal(
            barrier, inc=1, device_id={"mode": lax.rem(me + off, n)}, device_id_type=MESH
        )

    @pl.when(sp > 0)
    def _():
        pl.semaphore_signal(barrier, inc=1, device_id={"space": sp - 1}, device_id_type=MESH)

    @pl.when(sp < ns - 1)
    def _():
        pl.semaphore_signal(barrier, inc=1, device_id={"space": sp + 1}, device_id_type=MESH)

    @pl.when(sp == 0)
    def _():
        lo[...] = jnp.zeros_like(lo)

    @pl.when(sp == ns - 1)
    def _():
        hi[...] = jnp.zeros_like(hi)

    acc[...] = jnp.zeros_like(acc)
    acc2[...] = jnp.zeros_like(acc2)
    for copy in fetched:
        copy.wait()
    marks[...] = jnp.where(iota((width, rough), 0) == lax.rem(cells[...], width), 1.0, 0.0).astype(
        BF16
    )
    on_row[...] = jnp.where(iota((rows, rough), 0) == cells[...] // width, 1.0, 0.0)
    low = jnp.where(sp > 0, 1, 0)
    high = jnp.where(sp < ns - 1, 1, 0)
    pl.semaphore_wait(barrier, n - 1 + low + high)

    def down_copy(i):
        d, b = chunks[i]
        where = pl.ds(d * modes + b * batch, batch)
        return send(
            first.at[where], hi.at[where], hsem.at[0, i], hsem.at[1, i], "space",
            lax.rem(sp + ns - 1, ns),
        )

    def up_copy(i):
        d, b = chunks[i]
        where = pl.ds(d * modes + b * batch, batch)
        return send(
            last.at[where], lo.at[where], hsem.at[2, i], hsem.at[3, i], "space",
            lax.rem(sp + 1, ns),
        )

    def halo_wait(i):
        @pl.when(sp > 0)
        def _():
            down_copy(i).wait_send()
            up_copy(i).wait_recv()

        @pl.when(sp < ns - 1)
        def _():
            up_copy(i).wait_send()
            down_copy(i).wait_recv()

    def take(i):
        d, b = chunks[i]
        base = d * modes + b * batch
        load(i).wait()

        def edges(t, carry):
            p = base + t
            for z in range(planes):
                first[p, pl.ds(z, 1), :] = xv[p, pl.ds(z * rows, 1), :]
                last[p, pl.ds(z, 1), :] = xv[p, pl.ds((z + 1) * rows - 1, 1), :]
            return carry

        lax.fori_loop(0, batch, edges, 0)

        @pl.when(sp > 0)
        def _():
            down_copy(i).start()

        @pl.when(sp < ns - 1)
        def _():
            up_copy(i).start()

        w = weight[0, me * dirs + d]

        def add_rows(r, carry):
            here = pl.ds(pl.multiple_of(r * SUB, SUB), SUB)
            value = xv[base, here, :]
            for t in range(1, batch):
                value = value + xv[base + t, here, :]
            acc[here, :] += w * value
            return carry

        lax.fori_loop(0, total_rows // SUB, add_rows, 0)

    row, lane = iota((SUB, LANE), 0), iota((SUB, LANE), 1)
    places = tiles(rows, width)
    last_row, last_col = rows - SUB, width - LANE

    def factors(d, m):
        s = me * dirs + d
        v = velocity[0, m]
        turn = v * jnp.abs(dir_cos[2, s])
        inv = 1.0 / splat(1.0 + rate[0, m] + turn)
        return v * jnp.abs(dir_cos[0, s]), v * jnp.abs(dir_cos[1, s]), turn, inv

    halo_done = set()

    def sweep(d, start, stop):
        for i, (dd, b) in enumerate(chunks):
            if dd == d and b * batch < stop and start < (b + 1) * batch and i not in halo_done:
                halo_done.add(i)
                halo_wait(i)
        s = me * dirs + d
        w = weight[0, s]
        low_x, low_y = splat(dir_cos[0, s]) >= 0.0, splat(dir_cos[1, s]) >= 0.0
        shift_x = jnp.where(dir_cos[0, s] >= 0.0, 1, SUB - 1)
        shift_y = jnp.where(dir_cos[1, s] >= 0.0, 1, LANE - 1)
        head_x, tail_x = low_x & (row == 0), ~low_x & (row == SUB - 1)
        head_y, tail_y = low_y & (lane == 0), ~low_y & (lane == LANE - 1)
        wide = 2

        def some(g, carry):
            sets, before = [], []
            for t in range(wide):
                m = start + g * wide + t
                vx, vy, turn, inv = factors(d, m)
                ky = inv * vy
                sets.append((
                    d * modes + m, inv * (1.0 - vx - vy), inv * vx, inv * turn,
                    ky, jnp.where(head_y, 0.0, ky), jnp.where(tail_y, 0.0, ky),
                ))
                if d % 2 == 0:
                    before.append({
                        (r, c): smooth[pl.ds(r, SUB), pl.ds(c, LANE)]
                        * xv[(d + 1) * modes + m, pl.ds(r, SUB), pl.ds(c, LANE)]
                        for r, c in places
                    })
                else:
                    before.append(None)
            for z in range(planes) if d % 2 == 0 else reversed(range(planes)):
                sums = {}
                for t in range(wide):
                    p, k0, kx, kp, ky, ky_head, ky_tail = sets[t]
                    own = {
                        (r, c): xv[p, pl.ds(z * rows + r, SUB), pl.ds(c, LANE)] for r, c in places
                    }
                    side = {at: pltpu.roll(own[at], shift_x, 0) for at in places}
                    along = {at: pltpu.roll(own[at], shift_y, 1) for at in places}
                    now = {}
                    for r, c in places:
                        cols = pl.ds(c, LANE)
                        if r == 0:
                            under = jnp.broadcast_to(lo[p, pl.ds(z, 1), cols], (SUB, LANE))
                        else:
                            under = side[r - SUB, c]
                        if r == last_row:
                            over = jnp.broadcast_to(hi[p, pl.ds(z, 1), cols], (SUB, LANE))
                        else:
                            over = side[r + SUB, c]
                        one = jnp.where(head_x, under, jnp.where(tail_x, over, side[r, c]))
                        two = along[r, c]
                        if c > 0:
                            two = jnp.where(head_y, along[r, c - LANE], two)
                        if c < last_col:
                            two = jnp.where(tail_y, along[r, c + LANE], two)
                        gain = ky
                        if c == 0:
                            gain = ky_head
                        if c == last_col:
                            gain = ky_tail if c else jnp.where(tail_y, 0.0, ky_head)
                        value = k0 * own[r, c] + kx * one + gain * two
                        if before[t] is not None:
                            value = value + kp * before[t][r, c]
                        now[r, c] = value
                        xv[p, pl.ds(z * rows + r, SUB), cols] = value
                        sums[r, c] = sums[r, c] + value if t else value
                    before[t] = now
                for r, c in places:
                    acc2[pl.ds(z * rows + r, SUB), pl.ds(c, LANE)] += w * sums[r, c]
            return carry

        lax.fori_loop(0, (stop - start) // wide, some, 0)

    def settle(h, start, stop):
        wide = 2
        up, down = 2 * h, 2 * h + 1

        def some(g, carry):
            sets, values = [], []
            for t in range(wide):
                m = start + g * wide + t
                _, _, turn, inv = factors(up, m)
                sets.append((m, inv * turn, inv * (rate[0, m] * spectrum[0, m])))
                values.append({
                    (r, c): heat[pl.ds(r, SUB), pl.ds(c, LANE)] * spectrum[0, m] for r, c in places
                })
            for d, z in [(down, z) for z in reversed(range(planes))] + [
                (up, z) for z in range(planes)
            ]:
                for r, c in places:
                    here, cols = pl.ds(z * rows + r, SUB), pl.ds(c, LANE)
                    level = equil[here, cols]
                    for t in range(wide):
                        m, kp, ks = sets[t]
                        value = values[t][r, c]
                        if d == up and z == 0:
                            value = value * smooth[pl.ds(r, SUB), cols]
                        value = kp * value + ks * level
                        values[t][r, c] = value
                        xv[d * modes + m, here, cols] += value
            return carry

        lax.fori_loop(0, (stop - start) // wide, some, 0)

    def rows_of(way, part):
        return (2 * way + part) * piece

    def pair_of(q):
        return (2 * (q // modes) + 1) * modes + q % modes

    def at_slots(values):
        k = values.shape[0]
        high, low = split(values.reshape(k * rows, width))
        column = marks[...]
        got = dot(high, column) + dot(low, column)
        return jnp.sum(got.reshape(k, rows, rough) * on_row[...][None], axis=1)

    def gather(q):
        held[place, pl.ds(q, piece), :] = at_slots(
            xv[pl.ds(pair_of(q), piece), pl.ds(0, rows), :]
        )

    def slot_of(way, step):
        return lax.rem(place + n + (-step if way == 0 else step), n)

    def copy_of(way, part, step):
        at = held.at[slot_of(way, step), pl.ds(rows_of(way, part), piece)]
        return send(at, at, ssem.at[way, part, step], rsem.at[way, part, step], "mode", ends[way])

    def arrival(way, part, step):
        at = held.at[slot_of(way, step + 1), pl.ds(rows_of(way, part), piece)]
        return send(at, at, ssem.at[way, part, step], rsem.at[way, part, step], "mode", ends[way])

    def choose(way, step):
        slot = slot_of(way, step)
        owner = index_of(slot)
        q0 = rows_of(way, 0)
        block[...] = (
            held[slot, pl.ds(q0, 2 * piece), :]
            + lift[pl.ds(pl.multiple_of(owner * quiet + q0, SUB), 2 * piece), :]
        )
        j, m0 = owner * half + q0 // modes, q0 % modes

        def one(k, carry):
            hit = reflect[pl.ds(k, 1), :] == j
            for q in range(0, 2 * piece, SUB):
                here = pl.ds(pl.multiple_of(k * modes + m0 + q, SUB), SUB)
                picked[here, :] = jnp.where(hit, block[pl.ds(q, SUB), :], picked[here, :])
            return carry

        lax.fori_loop(0, ups, one, 0)

    def prepare():
        size, lanes = ups * modes, response.shape[1]
        which = iota((size, 1), 0)
        modal = iota((size, modes), 1) == lax.rem(which, modes)
        angle = iota((size, 2 * ups), 1) == 2 * (which // modes) + 1

        def spread(mask, values):
            return jnp.sum(jnp.where(mask, values, 0.0), axis=1, keepdims=True)

        v, e = spread(modal, velocity_row[...]), spread(modal, rate_row[...])
        f = spread(modal, spectrum_row[...])
        turn = v * spread(angle, jnp.abs(dir_row[pl.ds(2, 1), :]))
        inv = 1.0 / (1.0 + e + turn)
        kp, power = turn * inv, inv * (e * f)
        at = iota((size, lanes), 1)
        out = jnp.zeros((size, lanes), F32)
        for z in range(planes):
            out = jnp.where(at == z, power, out)
            power = power * kp
        power = f * kp
        for z in range(planes - 1):
            power = power * kp
        response[...] = jnp.where(at == planes, power, out)

    def raise_all():
        lanes = response.shape[1]
        levels = at_slots(equil[...].reshape(planes, rows, width))
        face = at_slots(heat[...].reshape(1, rows, width))
        spare = jnp.zeros((lanes - planes - 1, rough), F32)
        sources = jnp.concatenate([levels, face, spare], axis=0)
        lift[...] = fine_dot(response[...], sources)

    def find_rough():
        live[...] = jnp.where(iota((rows, rough), 1) < count[0], on_row[...], 0.0)
        rough_at = lax.dot_general(
            live[...].astype(BF16), marks[...], (((1,), (1,)), ((), ())), preferred_element_type=F32
        )
        smooth[...] = jnp.where(rough_at > 0.5, 0.0, 0.9)

    opening = Reduction(acc, slots1, part1, equil, sems1, n)
    closing = Reduction(acc2, slots2, part2, summed, sems2, n)
    n_down = half * per_dir

    def launch(way, part):
        q = rows_of(way, part)
        sweep(2 * (q // modes) + 1, q % modes, q % modes + piece)
        gather(q)
        copy_of(way, part, 0).start()

    for i in range(n_down):
        take(i)
    find_rough()
    prepare()
    for way in range(2):
        launch(way, 0)
    for i in range(n_down, len(chunks)):
        take(i)
    opening.start()
    for way in range(2):
        launch(way, 1)

    def middle():
        opening.combine(lambda value: squash(value * (1.0 / pairs_total)))

    def third():
        opening.finish()
        raise_all()

    tasks = []
    slices = [(h, m) for h in range(half) for m in range(0, modes, SUB)]
    for i, (h, m) in enumerate(slices):
        tasks.append(functools.partial(sweep, 2 * h, m, m + SUB))
        if i == 1:
            tasks.append(middle)
    tasks.append(closing.start)
    tasks.append(third)
    for i, (h, m) in enumerate(slices):
        tasks.append(functools.partial(settle, h, m, m + SUB))
        if i == len(slices) - 3:
            tasks.append(lambda: closing.combine(lambda value: value))
    picked[...] = jnp.zeros_like(picked)
    total = len(tasks) + 2 * n
    events = 4 * (n - 1)
    for way in range(2):
        tasks.append(functools.partial(choose, way, 0))
    done, seen = 0, 0
    for step in range(1, n):
        for part in range(2):
            for way in range(2):
                arrival(way, part, step - 1).wait_recv()
                if step < n - 1:
                    copy_of(way, part, step).start()
                if part == 1:
                    tasks.append(functools.partial(choose, way, step))
                seen += 1
                while tasks and done * events < total * seen:
                    tasks.pop(0)()
                    done += 1
    for task in tasks:
        task()
    closing.finish()
    for step in range(n - 1):
        for part in range(2):
            for way in range(2):
                copy_of(way, part, step).wait_send()


def main_step(scalars, count, heat, cells, reflect, x, n, ns, planes):
    pairs, total_rows, width = x.shape
    rows = total_rows // planes
    modes = scalars[1].shape[1]
    quiet = pairs // 2
    rough = cells.shape[1]
    every = reflect.shape[0] * modes
    n_chunks = (pairs // modes) * (modes // min(16, modes))
    flat = (total_rows, width)
    part = (total_rows // n, width)
    halo = pltpu.VMEM((pairs, planes, width), F32)
    lanes = -(-(planes + 1) // 16) * 16
    return pl.pallas_call(
        functools.partial(main_kernel, n, ns, planes),
        out_shape=(
            jax.ShapeDtypeStruct(x.shape, F32),
            jax.ShapeDtypeStruct((every, rough), F32),
            jax.ShapeDtypeStruct(flat, F32),
            jax.ShapeDtypeStruct(flat, F32),
            jax.ShapeDtypeStruct((rows, width), F32),
            jax.ShapeDtypeStruct((rows, rough), F32),
            jax.ShapeDtypeStruct((width, rough), BF16),
        ),
        in_specs=[whole(pltpu.SMEM)] + [whole(pltpu.HBM)] * 9,
        out_specs=(whole(),) * 7,
        scratch_shapes=[
            *(pltpu.SMEM(a.shape, a.dtype) for a in scalars),
            *(pltpu.VMEM(a.shape, a.dtype) for a in (*scalars[:4], heat, cells, reflect)),
            halo, halo, halo, halo,
            pltpu.VMEM(flat, F32),
            pltpu.VMEM((n, *part), F32),
            pltpu.VMEM(part, F32),
            pltpu.VMEM(flat, F32),
            pltpu.VMEM((n, *part), F32),
            pltpu.VMEM(part, F32),
            pltpu.VMEM((n, quiet, rough), F32),
            pltpu.VMEM((quiet // 2, rough), F32),
            pltpu.VMEM((every, rough), F32),
            pltpu.VMEM((rows, rough), F32),
            pltpu.VMEM((every, lanes), F32),
            pltpu.SemaphoreType.DMA((12,)),
            pltpu.SemaphoreType.DMA((n_chunks,)),
            pltpu.SemaphoreType.DMA((4, n_chunks)),
            pltpu.SemaphoreType.DMA((4, n)),
            pltpu.SemaphoreType.DMA((4, n)),
            pltpu.SemaphoreType.DMA((2, 2, n - 1)),
            pltpu.SemaphoreType.DMA((2, 2, n - 1)),
        ],
        compiler_params=pltpu.CompilerParams(
            collective_id=0, has_side_effects=True, vmem_limit_bytes=28 * MIB
        ),
        name="main_step",
    )(count, *in_hbm(*scalars, heat, cells, reflect, x))


def emit_kernel(
    planes, pairs_total, dir_cos_in, velocity_in, rate_in, spectrum_in, weight_in, heat_in,
    xv, picked, equil, summed, smooth, live, marks,
    out, energy,
    dir_cos, velocity, rate, dir_row, velocity_row, rate_row, spectrum_row, weight_row, heat,
    rising, inflow, gains, moments, psem, sem,
):
    pairs, total_rows, width = xv.shape
    rows = total_rows // planes
    modes = velocity.shape[1]
    dirs = pairs // modes
    half = dirs // 2
    every, rough = picked.shape
    batch = min(8, modes)
    me = lax.axis_index("mode")
    places = tiles(rows, width)

    def whole_dir(d):
        where = pl.ds(d * modes, modes)
        return pltpu.make_async_copy(xv.at[where], out.at[where], sem.at[d, 0])

    def piece(d, b):
        return pltpu.make_async_copy(
            rising.at[pl.ds(d // 2 * modes + b * batch, batch)],
            out.at[pl.ds(d * modes + b * batch, batch)], sem.at[d, b],
        )

    fetched = copies((
        (dir_cos_in, dir_cos), (velocity_in, velocity), (rate_in, rate), (dir_cos_in, dir_row),
        (velocity_in, velocity_row), (rate_in, rate_row), (spectrum_in, spectrum_row),
        (weight_in, weight_row), (heat_in, heat),
    ), psem)
    for copy in fetched:
        copy.start()
    for d in range(1, dirs, 2):
        whole_dir(d).start()
    for copy in fetched:
        copy.wait()

    group = min(16, modes)
    for d in range(0, dirs, 2):
        cz = jnp.abs(dir_cos[2, me * dirs + d])
        for g in range(modes // group):
            first = pl.multiple_of((me * half + d // 2) * modes + g * group, group)
            spread = picked[pl.ds(first, group), :][:, None, :] * live[...][None]
            put = turned_dot(spread.reshape(group * rows, rough), marks[...])
            inflow[...] = 0.9 * put.reshape(group, rows, width)
            for b in range(g * group // batch, (g + 1) * group // batch):
                def one(i, carry):
                    m = b * batch + i
                    turn = velocity[0, m] * cz
                    ratio = splat(turn) / splat(1.0 + rate[0, m] + turn)
                    for r, c in places:
                        cols = pl.ds(c, LANE)
                        value = inflow[m - g * group, pl.ds(r, SUB), cols]
                        for z in range(planes):
                            here = pl.ds(z * rows + r, SUB)
                            value = ratio * value
                            rising[d // 2 * modes + m, here, cols] = (
                                xv[d * modes + m, here, cols] + value
                            )
                    return carry

                lax.fori_loop(0, batch, one, 0)
                piece(d, b).start()

    n_dirs = weight_row.shape[1]

    def column(values):
        size = values.shape[1]
        same = iota((size, size), 0) == iota((size, size), 1)
        return jnp.sum(jnp.where(same, values, 0.0), axis=1, keepdims=True)

    which = iota((1, every), 1)

    def spread_over(values, index):
        size = values.shape[1]
        mask = iota((size, every), 0) == index
        return jnp.sum(jnp.where(mask, column(values), 0.0), axis=0, keepdims=True)

    modal, angle = lax.rem(which, modes), 2 * (which // modes)
    v, e = spread_over(velocity_row[...], modal), spread_over(rate_row[...], modal)
    f = spread_over(spectrum_row[...], modal)
    turn = v * spread_over(jnp.abs(dir_row[pl.ds(2, 1), :]), angle)
    w_up, w_down = spread_over(weight_row[...], angle), spread_over(weight_row[...], angle + 1)
    inv = 1.0 / (1.0 + e + turn)
    kp, ks = turn * inv, inv * (e * f)
    top = 2 * planes + 2
    power = jnp.ones_like(kp)
    for q in range(top):
        if 1 <= q <= planes:
            gains[pl.ds(q - 1, 1), :] = 0.9 * w_up * power
        for i, scale in enumerate((w_up * ks, w_down * ks, w_up * f, w_down * f)):
            total = jnp.sum(scale * power, axis=1, keepdims=True)
            moments[i, pl.ds(q, 1), :] = jnp.broadcast_to(total, (1, LANE))
        power = power * kp
    at_slot = fine_dot(gains[...], picked[...])
    spread = at_slot[:, None, :] * live[...][None]
    rough_part = turned_dot(spread.reshape(total_rows, rough), marks[...])

    def moment(i, q):
        return jnp.broadcast_to(moments[i, pl.ds(q, 1), :], (SUB, LANE))

    for r, c in places:
        cols = pl.ds(c, LANE)
        levels = [equil[pl.ds(z * rows + r, SUB), cols] for z in range(planes)]
        face = heat[pl.ds(r, SUB), cols]
        plain = smooth[pl.ds(r, SUB), cols]
        for z in range(planes):
            here = pl.ds(z * rows + r, SUB)
            value = summed[here, cols] + rough_part[z * rows + r : z * rows + r + SUB, c : c + LANE]
            value = value + moment(3, planes - z) * face
            turned = moment(2, z + 1 + planes) * face
            for y in range(planes):
                if y <= z:
                    value = value + moment(0, z - y) * levels[y]
                if y >= z:
                    value = value + moment(1, y - z) * levels[y]
                turned = turned + moment(0, z + 1 + y) * levels[y]
            energy[here, cols] = (value + plain * turned) * (1.0 / pairs_total)
    for d in range(dirs):
        if d % 2:
            whole_dir(d).wait()
        else:
            for b in range(modes // batch):
                piece(d, b).wait()


def emit_step(planes, pairs_total, scalars, heat, parts):
    xv, picked = parts[:2]
    pairs, total_rows, width = xv.shape
    modes = scalars[1].shape[1]
    rows = total_rows // planes
    return pl.pallas_call(
        functools.partial(emit_kernel, planes, pairs_total),
        out_shape=(
            jax.ShapeDtypeStruct(xv.shape, F32),
            jax.ShapeDtypeStruct((total_rows, width), F32),
        ),
        in_specs=[whole(pltpu.HBM)] * 6 + [whole()] * len(parts),
        out_specs=(whole(pltpu.HBM), whole()),
        scratch_shapes=[
            *(pltpu.SMEM(a.shape, a.dtype) for a in scalars[:3]),
            *(pltpu.VMEM(a.shape, a.dtype) for a in (*scalars, heat)),
            pltpu.VMEM((pairs // 2, total_rows, width), F32),
            pltpu.VMEM((min(16, modes), rows, width), F32),
            pltpu.VMEM((planes, picked.shape[0]), F32),
            pltpu.VMEM((4, -(-(2 * planes + 2) // SUB) * SUB, LANE), F32),
            pltpu.SemaphoreType.DMA((9,)),
            pltpu.SemaphoreType.DMA((pairs // modes, modes // min(8, modes))),
        ],
        compiler_params=pltpu.CompilerParams(vmem_limit_bytes=28 * MIB),
        name="emit_step",
    )(*in_hbm(*scalars, heat), *parts)


def per_device(
    n, ns, intensity, dir_cos, velocity, rate, spectrum, weight, heat, rough_cells, rough_count,
    rough_map,
):
    pairs, planes, rows, width = intensity.shape
    x = intensity.reshape(pairs, planes * rows, width)
    scalars = (dir_cos, velocity[None], rate[None], spectrum[None], weight[None])
    parts = main_step(scalars, rough_count, heat, rough_cells[None], rough_map.T, x, n, ns, planes)
    fresh, energy = emit_step(planes, pairs * n, scalars, heat, parts)
    return fresh.reshape(intensity.shape), energy.reshape(planes, rows, width)


def solution(mesh):
    n, ns = mesh.shape["mode"], mesh.shape["space"]
    in_specs = (
        P("mode", None, "space", None),
        P(),
        P(),
        P(),
        P(),
        P(),
        P("space", None),
        P("space"),
        P("space"),
        P("space", None),
    )
    out_specs = (P("mode", None, "space", None), P(None, "space", None))
    return jax.shard_map(
        functools.partial(per_device, n, ns),
        mesh=mesh,
        in_specs=in_specs,
        out_specs=out_specs,
        check_vma=False,
    )
```

```python
import functools

import jax
import jax.numpy as jnp
from jax import lax
from jax.experimental import pallas as pl
from jax.experimental.pallas import tpu as pltpu
from jax.sharding import PartitionSpec as P

MESH = pl.DeviceIdType.MESH
F32 = jnp.float32
BF16 = jnp.bfloat16
SUB, LANE = 8, 128
MIB = 1 << 20


def whole(space=pltpu.VMEM):
    return pl.BlockSpec(memory_space=space)


def in_hbm(*arrays):
    return tuple(pltpu.with_memory_space_constraint(a, pltpu.HBM) for a in arrays)


def squash(energy):
    return energy / (1.0 + 0.3 * jnp.abs(energy))


def send(src, dst, ssem, rsem, axis, target):
    return pltpu.make_async_remote_copy(
        src_ref=src,
        dst_ref=dst,
        send_sem=ssem,
        recv_sem=rsem,
        device_id={axis: target},
        device_id_type=MESH,
    )


class Reduction:
    def __init__(self, acc, slots, part, total, sems, n):
        self.acc, self.slots, self.part, self.total = acc, slots, part, total
        self.sems, self.n = sems, n
        self.me = lax.axis_index("mode")
        self.rows = acc.shape[0] // n

    def chunk(self, i):
        return pl.ds(pl.multiple_of(i * self.rows, self.rows), self.rows)

    def outward(self, off):
        target = lax.rem(self.me + off, self.n)
        return send(
            self.acc.at[self.chunk(target)], self.slots.at[off],
            self.sems.at[0, off], self.sems.at[1, off], "mode", target,
        )

    def spread(self, off):
        target = lax.rem(self.me + off, self.n)
        return send(
            self.part, self.total.at[self.chunk(self.me)],
            self.sems.at[2, off], self.sems.at[3, off], "mode", target,
        )

    def start(self):
        for off in range(1, self.n):
            self.outward(off).start()

    def combine(self, finish):
        for off in range(1, self.n):
            self.outward(off).wait_recv()
        value = self.acc[self.chunk(self.me), :]
        for off in range(1, self.n):
            value = value + self.slots[off]
        self.part[...] = finish(value)
        for off in range(1, self.n):
            self.spread(off).start()
        self.total[self.chunk(self.me), :] = self.part[...]

    def finish(self):
        for off in range(1, self.n):
            source = lax.rem(self.me + self.n - off, self.n)
            send(
                self.part, self.total.at[self.chunk(source)],
                self.sems.at[2, off], self.sems.at[3, off], "mode", source,
            ).wait_recv()
        for off in range(1, self.n):
            self.outward(off).wait_send()
            self.spread(off).wait_send()


def split(value):
    high = value.astype(BF16)
    return high, (value - high.astype(F32)).astype(BF16)


def splat(value):
    return jnp.full((SUB, LANE), value, F32)


def tiles(rows, width):
    return [(r, c) for r in range(0, rows, SUB) for c in range(0, width, LANE)]


def dot(a, b):
    return jnp.dot(a, b, preferred_element_type=F32)


def fine_dot(a, b):
    a_high, a_low = split(a)
    b_high, b_low = split(b)
    return dot(a_high, b_high) + (dot(a_high, b_low) + dot(a_low, b_high))


def turned_dot(a, b):
    contract = (((1,), (1,)), ((), ()))
    high, low = split(a)
    return lax.dot_general(high, b, contract, preferred_element_type=F32) + lax.dot_general(
        low, b, contract, preferred_element_type=F32
    )


def iota(shape, axis):
    return lax.broadcasted_iota(jnp.int32, shape, axis)


def copies(pairs, sem):
    return [pltpu.make_async_copy(src, dst, sem.at[i]) for i, (src, dst) in enumerate(pairs)]


def main_kernel(
    n, ns, planes,
    count, dir_cos_in, velocity_in, rate_in, spectrum_in, weight_in, heat_in, cells_in, reflect_in,
    x,
    xv, returned, glow, equil, summed, smooth, live, marks,
    dir_cos, velocity, rate, spectrum, weight, dir_row, velocity_row, rate_row, spectrum_row,
    weight_row, heat, cells, reflect,
    lo, hi, first, last, acc, slots1, part1, acc2, slots2, part2,
    outbox, inbox, wanted, picked, shine, on_row, response, gains,
    psem, lsem, hsem, sems1, sems2, gone, come, back_gone, back_come,
):
    me, sp = lax.axis_index("mode"), lax.axis_index("space")
    pairs, total_rows, width = xv.shape
    rows = total_rows // planes
    modes = velocity.shape[1]
    dirs = pairs // modes
    half = dirs // 2
    quiet = half * modes
    ups = reflect.shape[0]
    pairs_total = pairs * n
    rough = cells.shape[1]
    share = rough // n
    piece = quiet // 4
    batch = min(16, modes)
    per_dir = modes // batch
    order = [d for d in range(1, dirs, 2)] + [d for d in range(0, dirs, 2)]
    chunks = [(d, b) for d in order for b in range(per_dir)]

    fetched = copies((
        (cells_in, cells), (weight_in, weight), (dir_cos_in, dir_cos), (velocity_in, velocity),
        (rate_in, rate), (spectrum_in, spectrum), (dir_cos_in, dir_row),
        (velocity_in, velocity_row), (rate_in, rate_row), (spectrum_in, spectrum_row),
        (weight_in, weight_row), (heat_in, heat), (reflect_in, reflect),
    ), psem)
    for copy in fetched:
        copy.start()

    def load(i):
        d, b = chunks[i]
        where = pl.ds(d * modes + b * batch, batch)
        return pltpu.make_async_copy(x.at[where], xv.at[where], lsem.at[i])

    for i in range(len(chunks)):
        load(i).start()

    barrier = pltpu.get_barrier_semaphore()
    for off in range(1, n):
        pl.semaphore_signal(
            barrier, inc=1, device_id={"mode": lax.rem(me + off, n)}, device_id_type=MESH
        )

    @pl.when(sp > 0)
    def _():
        pl.semaphore_signal(barrier, inc=1, device_id={"space": sp - 1}, device_id_type=MESH)

    @pl.when(sp < ns - 1)
    def _():
        pl.semaphore_signal(barrier, inc=1, device_id={"space": sp + 1}, device_id_type=MESH)

    @pl.when(sp == 0)
    def _():
        lo[...] = jnp.zeros_like(lo)

    @pl.when(sp == ns - 1)
    def _():
        hi[...] = jnp.zeros_like(hi)

    acc[...] = jnp.zeros_like(acc)
    acc2[...] = jnp.zeros_like(acc2)
    for copy in fetched:
        copy.wait()
    marks[...] = jnp.where(iota((width, rough), 0) == lax.rem(cells[...], width), 1.0, 0.0).astype(
        BF16
    )
    on_row[...] = jnp.where(iota((rows, rough), 0) == cells[...] // width, 1.0, 0.0)
    low = jnp.where(sp > 0, 1, 0)
    high = jnp.where(sp < ns - 1, 1, 0)
    pl.semaphore_wait(barrier, n - 1 + low + high)

    def down_copy(i):
        d, b = chunks[i]
        where = pl.ds(d * modes + b * batch, batch)
        return send(
            first.at[where], hi.at[where], hsem.at[0, i], hsem.at[1, i], "space",
            lax.rem(sp + ns - 1, ns),
        )

    def up_copy(i):
        d, b = chunks[i]
        where = pl.ds(d * modes + b * batch, batch)
        return send(
            last.at[where], lo.at[where], hsem.at[2, i], hsem.at[3, i], "space",
            lax.rem(sp + 1, ns),
        )

    def halo_wait(i):
        @pl.when(sp > 0)
        def _():
            down_copy(i).wait_send()
            up_copy(i).wait_recv()

        @pl.when(sp < ns - 1)
        def _():
            up_copy(i).wait_send()
            down_copy(i).wait_recv()

    def take(i):
        d, b = chunks[i]
        base = d * modes + b * batch
        load(i).wait()

        def edges(t, carry):
            p = base + t
            for z in range(planes):
                first[p, pl.ds(z, 1), :] = xv[p, pl.ds(z * rows, 1), :]
                last[p, pl.ds(z, 1), :] = xv[p, pl.ds((z + 1) * rows - 1, 1), :]
            return carry

        lax.fori_loop(0, batch, edges, 0)

        @pl.when(sp > 0)
        def _():
            down_copy(i).start()

        @pl.when(sp < ns - 1)
        def _():
            up_copy(i).start()

        w = weight[0, me * dirs + d]

        def add_rows(r, carry):
            here = pl.ds(pl.multiple_of(r * SUB, SUB), SUB)
            value = xv[base, here, :]
            for t in range(1, batch):
                value = value + xv[base + t, here, :]
            acc[here, :] += w * value
            return carry

        lax.fori_loop(0, total_rows // SUB, add_rows, 0)

    row, lane = iota((SUB, LANE), 0), iota((SUB, LANE), 1)
    places = tiles(rows, width)
    last_row, last_col = rows - SUB, width - LANE

    def factors(d, m):
        s = me * dirs + d
        v = velocity[0, m]
        turn = v * jnp.abs(dir_cos[2, s])
        inv = 1.0 / splat(1.0 + rate[0, m] + turn)
        return v * jnp.abs(dir_cos[0, s]), v * jnp.abs(dir_cos[1, s]), turn, inv

    halo_done = set()

    def sweep(d, start, stop):
        for i, (dd, b) in enumerate(chunks):
            if dd == d and b * batch < stop and start < (b + 1) * batch and i not in halo_done:
                halo_done.add(i)
                halo_wait(i)
        s = me * dirs + d
        w = weight[0, s]
        low_x, low_y = splat(dir_cos[0, s]) >= 0.0, splat(dir_cos[1, s]) >= 0.0
        shift_x = jnp.where(dir_cos[0, s] >= 0.0, 1, SUB - 1)
        shift_y = jnp.where(dir_cos[1, s] >= 0.0, 1, LANE - 1)
        head_x, tail_x = low_x & (row == 0), ~low_x & (row == SUB - 1)
        head_y, tail_y = low_y & (lane == 0), ~low_y & (lane == LANE - 1)
        wide = 2

        def some(g, carry):
            sets, before = [], []
            for t in range(wide):
                m = start + g * wide + t
                vx, vy, turn, inv = factors(d, m)
                ky = inv * vy
                sets.append((
                    d * modes + m, inv * (1.0 - vx - vy), inv * vx, inv * turn,
                    ky, jnp.where(head_y, 0.0, ky), jnp.where(tail_y, 0.0, ky),
                ))
                if d % 2 == 0:
                    before.append({
                        (r, c): smooth[pl.ds(r, SUB), pl.ds(c, LANE)]
                        * xv[(d + 1) * modes + m, pl.ds(r, SUB), pl.ds(c, LANE)]
                        for r, c in places
                    })
                else:
                    before.append(None)
            for z in range(planes) if d % 2 == 0 else reversed(range(planes)):
                sums = {}
                for t in range(wide):
                    p, k0, kx, kp, ky, ky_head, ky_tail = sets[t]
                    own = {
                        (r, c): xv[p, pl.ds(z * rows + r, SUB), pl.ds(c, LANE)] for r, c in places
                    }
                    side = {at: pltpu.roll(own[at], shift_x, 0) for at in places}
                    along = {at: pltpu.roll(own[at], shift_y, 1) for at in places}
                    now = {}
                    for r, c in places:
                        cols = pl.ds(c, LANE)
                        if r == 0:
                            under = jnp.broadcast_to(lo[p, pl.ds(z, 1), cols], (SUB, LANE))
                        else:
                            under = side[r - SUB, c]
                        if r == last_row:
                            over = jnp.broadcast_to(hi[p, pl.ds(z, 1), cols], (SUB, LANE))
                        else:
                            over = side[r + SUB, c]
                        one = jnp.where(head_x, under, jnp.where(tail_x, over, side[r, c]))
                        two = along[r, c]
                        if c > 0:
                            two = jnp.where(head_y, along[r, c - LANE], two)
                        if c < last_col:
                            two = jnp.where(tail_y, along[r, c + LANE], two)
                        gain = ky
                        if c == 0:
                            gain = ky_head
                        if c == last_col:
                            gain = ky_tail if c else jnp.where(tail_y, 0.0, ky_head)
                        value = k0 * own[r, c] + kx * one + gain * two
                        if before[t] is not None:
                            value = value + kp * before[t][r, c]
                        now[r, c] = value
                        xv[p, pl.ds(z * rows + r, SUB), cols] = value
                        sums[r, c] = sums[r, c] + value if t else value
                    before[t] = now
                for r, c in places:
                    acc2[pl.ds(z * rows + r, SUB), pl.ds(c, LANE)] += w * sums[r, c]
            return carry

        lax.fori_loop(0, (stop - start) // wide, some, 0)

    def settle(h, start, stop):
        wide = 2
        up, down = 2 * h, 2 * h + 1

        def some(g, carry):
            sets, values = [], []
            for t in range(wide):
                m = start + g * wide + t
                _, _, turn, inv = factors(up, m)
                sets.append((m, inv * turn, inv * (rate[0, m] * spectrum[0, m])))
                values.append({
                    (r, c): heat[pl.ds(r, SUB), pl.ds(c, LANE)] * spectrum[0, m] for r, c in places
                })
            for d, z in [(down, z) for z in reversed(range(planes))] + [
                (up, z) for z in range(planes)
            ]:
                for r, c in places:
                    here, cols = pl.ds(z * rows + r, SUB), pl.ds(c, LANE)
                    level = equil[here, cols]
                    for t in range(wide):
                        m, kp, ks = sets[t]
                        value = values[t][r, c]
                        if d == up and z == 0:
                            value = value * smooth[pl.ds(r, SUB), cols]
                        value = kp * value + ks * level
                        values[t][r, c] = value
                        xv[d * modes + m, here, cols] += value
            return carry

        lax.fori_loop(0, (stop - start) // wide, some, 0)

    def pair_of(q):
        return (2 * (q // modes) + 1) * modes + q % modes

    def at_slots(values):
        k = values.shape[0]
        high, low = split(values.reshape(k * rows, width))
        column = marks[...]
        got = dot(high, column) + dot(low, column)
        return jnp.sum(got.reshape(k, rows, rough) * on_row[...][None], axis=1)

    def shares(values):
        return [values[:, i * share : (i + 1) * share] for i in range(n)]

    def outward(part, off):
        target = lax.rem(me + off, n)
        here = pl.ds(part * piece, piece)
        return send(
            outbox.at[target, here], inbox.at[me, here], gone.at[part, off], come.at[part, off],
            "mode", target,
        )

    def arrival(part, off):
        source = lax.rem(me + n - off, n)
        here = pl.ds(part * piece, piece)
        return send(
            outbox.at[source, here], inbox.at[source, here], gone.at[part, off],
            come.at[part, off], "mode", source,
        )

    def homeward(off):
        target = lax.rem(me + off, n)
        mine = pl.ds(pl.multiple_of(target * quiet, quiet), quiet)
        return [
            send(
                picked.at[mine], returned.at[me], back_gone.at[0, off], back_come.at[0, off],
                "mode", target,
            ),
            send(shine, glow.at[me], back_gone.at[1, off], back_come.at[1, off], "mode", target),
        ]

    def return_of(off):
        source = lax.rem(me + n - off, n)
        mine = pl.ds(pl.multiple_of(me * quiet, quiet), quiet)
        return [
            send(
                picked.at[mine], returned.at[source], back_gone.at[0, off], back_come.at[0, off],
                "mode", source,
            ),
            send(
                shine, glow.at[source], back_gone.at[1, off], back_come.at[1, off], "mode", source
            ),
        ]

    def launch(part):
        q = part * piece
        sweep(2 * (q // modes) + 1, q % modes, q % modes + piece)
        got = at_slots(xv[pl.ds(pair_of(q), piece), pl.ds(0, rows), :])
        for i, value in enumerate(shares(got)):
            outbox[i, pl.ds(q, piece), :] = value
        for off in range(1, n):
            outward(part, off).start()
        inbox[me, pl.ds(q, piece), :] = outbox[me, pl.ds(q, piece), :]

    def own_share(values):
        total = jnp.zeros((values.shape[0], share), values.dtype)
        for i, value in enumerate(shares(values)):
            total = jnp.where(me == i, value, total)
        return total

    def choose():
        for part in range(4):
            for off in range(1, n):
                arrival(part, off).wait_recv()
        lanes = response.shape[1]
        levels = at_slots(equil[...].reshape(planes, rows, width))
        face = at_slots(heat[...].reshape(1, rows, width))
        spare = jnp.zeros((lanes - planes - 1, rough), F32)
        sources = own_share(jnp.concatenate([levels, face, spare], axis=0))
        lift = fine_dot(response[...], sources)
        inbox[...] += lift.reshape(n, quiet, share)
        wanted[...] = own_share(reflect[...])

        def one(k, carry):
            want = wanted[pl.ds(k, 1), :]
            value = None
            for j in range(ups):
                source = inbox[j // half, pl.ds((j % half) * modes, modes), :]
                value = source if j == 0 else jnp.where(want == j, source, value)
            picked[pl.ds(pl.multiple_of(k * modes, modes), modes), :] = value
            return carry

        lax.fori_loop(0, ups, one, 0)
        shine[...] = fine_dot(gains[...], picked[...])
        for off in range(1, n):
            for copy in homeward(off):
                copy.start()
        returned[me] = picked[pl.ds(pl.multiple_of(me * quiet, quiet), quiet), :]
        glow[me] = shine[...]

    def prepare():
        size, lanes = ups * modes, response.shape[1]
        which = iota((size, 1), 0)
        modal = iota((size, modes), 1) == lax.rem(which, modes)
        angle = iota((size, 2 * ups), 1) == 2 * (which // modes) + 1

        def spread(mask, values):
            return jnp.sum(jnp.where(mask, values, 0.0), axis=1, keepdims=True)

        v, e = spread(modal, velocity_row[...]), spread(modal, rate_row[...])
        f = spread(modal, spectrum_row[...])
        turn = v * spread(angle, jnp.abs(dir_row[pl.ds(2, 1), :]))
        inv = 1.0 / (1.0 + e + turn)
        kp, power = turn * inv, inv * (e * f)
        at = iota((size, lanes), 1)
        out = jnp.zeros((size, lanes), F32)
        for z in range(planes):
            out = jnp.where(at == z, power, out)
            power = power * kp
        power = f * kp
        for z in range(planes - 1):
            power = power * kp
        response[...] = jnp.where(at == planes, power, out)

        which = iota((1, size), 1)

        def along(values, index):
            length = values.shape[1]
            same = iota((length, length), 0) == iota((length, length), 1)
            column = jnp.sum(jnp.where(same, values, 0.0), axis=1, keepdims=True)
            mask = iota((length, size), 0) == index
            return jnp.sum(jnp.where(mask, column, 0.0), axis=0, keepdims=True)

        modal, angle = lax.rem(which, modes), 2 * (which // modes)
        v, e = along(velocity_row[...], modal), along(rate_row[...], modal)
        turn = v * along(jnp.abs(dir_row[pl.ds(2, 1), :]), angle)
        kp = turn / (1.0 + e + turn)
        power = 0.9 * along(weight_row[...], angle)
        for z in range(planes):
            power = power * kp
            gains[pl.ds(z, 1), :] = power

    def find_rough():
        live[...] = jnp.where(iota((rows, rough), 1) < count[0], on_row[...], 0.0)
        rough_at = lax.dot_general(
            live[...].astype(BF16), marks[...], (((1,), (1,)), ((), ())), preferred_element_type=F32
        )
        smooth[...] = jnp.where(rough_at > 0.5, 0.0, 0.9)

    opening = Reduction(acc, slots1, part1, equil, sems1, n)
    closing = Reduction(acc2, slots2, part2, summed, sems2, n)
    n_down = half * per_dir

    for i in range(n_down):
        take(i)
    for part in range(2):
        launch(part)
    for i in range(n_down, len(chunks)):
        take(i)
    opening.start()
    for part in range(2, 4):
        launch(part)
    find_rough()
    slices = [(h, m) for h in range(half) for m in range(0, modes, SUB)]
    early = min(2, len(slices) - 1)
    for h, m in slices[:early]:
        sweep(2 * h, m, m + SUB)
    opening.combine(lambda value: squash(value * (1.0 / pairs_total)))
    prepare()
    middle = min(6, len(slices) - 1)
    for h, m in slices[early:middle]:
        sweep(2 * h, m, m + SUB)
    opening.finish()
    choose()
    for h, m in slices[middle:]:
        sweep(2 * h, m, m + SUB)
    closing.start()
    for i, (h, m) in enumerate(slices):
        settle(h, m, m + SUB)
        if i == len(slices) // 2:
            closing.combine(lambda value: value)
    closing.finish()
    for off in range(1, n):
        for copy in return_of(off):
            copy.wait_recv()
    for off in range(1, n):
        for part in range(4):
            outward(part, off).wait_send()
        for copy in homeward(off):
            copy.wait_send()


def main_step(scalars, count, heat, cells, reflect, x, n, ns, planes):
    pairs, total_rows, width = x.shape
    rows = total_rows // planes
    modes = scalars[1].shape[1]
    quiet = pairs // 2
    rough = cells.shape[1]
    every = reflect.shape[0] * modes
    share = rough // n
    n_chunks = (pairs // modes) * (modes // min(16, modes))
    flat = (total_rows, width)
    part = (total_rows // n, width)
    halo = pltpu.VMEM((pairs, planes, width), F32)
    lanes = -(-(planes + 1) // 16) * 16
    return pl.pallas_call(
        functools.partial(main_kernel, n, ns, planes),
        out_shape=(
            jax.ShapeDtypeStruct(x.shape, F32),
            jax.ShapeDtypeStruct((n, quiet, share), F32),
            jax.ShapeDtypeStruct((n, planes, share), F32),
            jax.ShapeDtypeStruct(flat, F32),
            jax.ShapeDtypeStruct(flat, F32),
            jax.ShapeDtypeStruct((rows, width), F32),
            jax.ShapeDtypeStruct((rows, rough), F32),
            jax.ShapeDtypeStruct((width, rough), BF16),
        ),
        in_specs=[whole(pltpu.SMEM)] + [whole(pltpu.HBM)] * 9,
        out_specs=(whole(),) * 8,
        scratch_shapes=[
            *(pltpu.SMEM(a.shape, a.dtype) for a in scalars),
            *(pltpu.VMEM(a.shape, a.dtype) for a in (*scalars, heat, cells, reflect)),
            halo, halo, halo, halo,
            pltpu.VMEM(flat, F32),
            pltpu.VMEM((n, *part), F32),
            pltpu.VMEM(part, F32),
            pltpu.VMEM(flat, F32),
            pltpu.VMEM((n, *part), F32),
            pltpu.VMEM(part, F32),
            pltpu.VMEM((n, quiet, share), F32),
            pltpu.VMEM((n, quiet, share), F32),
            pltpu.VMEM((reflect.shape[0], share), jnp.int32),
            pltpu.VMEM((every, share), F32),
            pltpu.VMEM((planes, share), F32),
            pltpu.VMEM((rows, rough), F32),
            pltpu.VMEM((every, lanes), F32),
            pltpu.VMEM((planes, every), F32),
            pltpu.SemaphoreType.DMA((13,)),
            pltpu.SemaphoreType.DMA((n_chunks,)),
            pltpu.SemaphoreType.DMA((4, n_chunks)),
            pltpu.SemaphoreType.DMA((4, n)),
            pltpu.SemaphoreType.DMA((4, n)),
            pltpu.SemaphoreType.DMA((4, n)),
            pltpu.SemaphoreType.DMA((4, n)),
            pltpu.SemaphoreType.DMA((2, n)),
            pltpu.SemaphoreType.DMA((2, n)),
        ],
        compiler_params=pltpu.CompilerParams(
            collective_id=0, has_side_effects=True, vmem_limit_bytes=28 * MIB
        ),
        name="main_step",
    )(count, *in_hbm(*scalars, heat, cells, reflect, x))


def emit_kernel(
    planes, pairs_total, dir_cos_in, velocity_in, rate_in, spectrum_in, weight_in, heat_in,
    xv, returned, glow, equil, summed, smooth, live, marks,
    out, energy,
    dir_cos, velocity, rate, dir_row, velocity_row, rate_row, spectrum_row, weight_row, heat,
    rising, inflow, moments, psem, sem,
):
    pairs, total_rows, width = xv.shape
    rows = total_rows // planes
    modes = velocity.shape[1]
    dirs = pairs // modes
    half = dirs // 2
    rough = live.shape[1]
    n = returned.shape[0]
    every = n * half * modes
    batch = min(8, modes)
    me = lax.axis_index("mode")
    places = tiles(rows, width)

    def whole_dir(d):
        where = pl.ds(d * modes, modes)
        return pltpu.make_async_copy(xv.at[where], out.at[where], sem.at[d, 0])

    def piece(d, b):
        return pltpu.make_async_copy(
            rising.at[pl.ds(d // 2 * modes + b * batch, batch)],
            out.at[pl.ds(d * modes + b * batch, batch)], sem.at[d, b],
        )

    fetched = copies((
        (dir_cos_in, dir_cos), (velocity_in, velocity), (rate_in, rate), (dir_cos_in, dir_row),
        (velocity_in, velocity_row), (rate_in, rate_row), (spectrum_in, spectrum_row),
        (weight_in, weight_row), (heat_in, heat),
    ), psem)
    for copy in fetched:
        copy.start()
    for d in range(1, dirs, 2):
        whole_dir(d).start()
    for copy in fetched:
        copy.wait()

    group = min(16, modes)
    for d in range(0, dirs, 2):
        cz = jnp.abs(dir_cos[2, me * dirs + d])
        for g in range(modes // group):
            first = pl.ds(d // 2 * modes + g * group, group)
            own = jnp.concatenate([returned[i, first, :] for i in range(n)], axis=1)
            spread = own[:, None, :] * live[...][None]
            put = turned_dot(spread.reshape(group * rows, rough), marks[...])
            inflow[...] = 0.9 * put.reshape(group, rows, width)
            for b in range(g * group // batch, (g + 1) * group // batch):
                def one(i, carry):
                    m = b * batch + i
                    turn = velocity[0, m] * cz
                    ratio = splat(turn) / splat(1.0 + rate[0, m] + turn)
                    for r, c in places:
                        cols = pl.ds(c, LANE)
                        value = inflow[m - g * group, pl.ds(r, SUB), cols]
                        for z in range(planes):
                            here = pl.ds(z * rows + r, SUB)
                            value = ratio * value
                            rising[d // 2 * modes + m, here, cols] = (
                                xv[d * modes + m, here, cols] + value
                            )
                    return carry

                lax.fori_loop(0, batch, one, 0)
                piece(d, b).start()

    n_dirs = weight_row.shape[1]

    def column(values):
        size = values.shape[1]
        same = iota((size, size), 0) == iota((size, size), 1)
        return jnp.sum(jnp.where(same, values, 0.0), axis=1, keepdims=True)

    which = iota((1, every), 1)

    def spread_over(values, index):
        size = values.shape[1]
        mask = iota((size, every), 0) == index
        return jnp.sum(jnp.where(mask, column(values), 0.0), axis=0, keepdims=True)

    modal, angle = lax.rem(which, modes), 2 * (which // modes)
    v, e = spread_over(velocity_row[...], modal), spread_over(rate_row[...], modal)
    f = spread_over(spectrum_row[...], modal)
    turn = v * spread_over(jnp.abs(dir_row[pl.ds(2, 1), :]), angle)
    w_up, w_down = spread_over(weight_row[...], angle), spread_over(weight_row[...], angle + 1)
    inv = 1.0 / (1.0 + e + turn)
    kp, ks = turn * inv, inv * (e * f)
    top = 2 * planes + 2
    power = jnp.ones_like(kp)
    for q in range(top):
        for i, scale in enumerate((w_up * ks, w_down * ks, w_up * f, w_down * f)):
            total = jnp.sum(scale * power, axis=1, keepdims=True)
            moments[i, pl.ds(q, 1), :] = jnp.broadcast_to(total, (1, LANE))
        power = power * kp
    at_slot = jnp.concatenate([glow[i] for i in range(n)], axis=1)
    spread = at_slot[:, None, :] * live[...][None]
    rough_part = turned_dot(spread.reshape(total_rows, rough), marks[...])

    def moment(i, q):
        return jnp.broadcast_to(moments[i, pl.ds(q, 1), :], (SUB, LANE))

    for r, c in places:
        cols = pl.ds(c, LANE)
        levels = [equil[pl.ds(z * rows + r, SUB), cols] for z in range(planes)]
        face = heat[pl.ds(r, SUB), cols]
        plain = smooth[pl.ds(r, SUB), cols]
        for z in range(planes):
            here = pl.ds(z * rows + r, SUB)
            value = summed[here, cols] + rough_part[z * rows + r : z * rows + r + SUB, c : c + LANE]
            value = value + moment(3, planes - z) * face
            turned = moment(2, z + 1 + planes) * face
            for y in range(planes):
                if y <= z:
                    value = value + moment(0, z - y) * levels[y]
                if y >= z:
                    value = value + moment(1, y - z) * levels[y]
                turned = turned + moment(0, z + 1 + y) * levels[y]
            energy[here, cols] = (value + plain * turned) * (1.0 / pairs_total)
    for d in range(dirs):
        if d % 2:
            whole_dir(d).wait()
        else:
            for b in range(modes // batch):
                piece(d, b).wait()


def emit_step(planes, pairs_total, scalars, heat, parts):
    xv = parts[0]
    pairs, total_rows, width = xv.shape
    modes = scalars[1].shape[1]
    rows = total_rows // planes
    return pl.pallas_call(
        functools.partial(emit_kernel, planes, pairs_total),
        out_shape=(
            jax.ShapeDtypeStruct(xv.shape, F32),
            jax.ShapeDtypeStruct((total_rows, width), F32),
        ),
        in_specs=[whole(pltpu.HBM)] * 6 + [whole()] * len(parts),
        out_specs=(whole(pltpu.HBM), whole()),
        scratch_shapes=[
            *(pltpu.SMEM(a.shape, a.dtype) for a in scalars[:3]),
            *(pltpu.VMEM(a.shape, a.dtype) for a in (*scalars, heat)),
            pltpu.VMEM((pairs // 2, total_rows, width), F32),
            pltpu.VMEM((min(16, modes), rows, width), F32),
            pltpu.VMEM((4, -(-(2 * planes + 2) // SUB) * SUB, LANE), F32),
            pltpu.SemaphoreType.DMA((9,)),
            pltpu.SemaphoreType.DMA((pairs // modes, modes // min(8, modes))),
        ],
        compiler_params=pltpu.CompilerParams(vmem_limit_bytes=28 * MIB),
        name="emit_step",
    )(*in_hbm(*scalars, heat), *parts)


def per_device(
    n, ns, intensity, dir_cos, velocity, rate, spectrum, weight, heat, rough_cells, rough_count,
    rough_map,
):
    pairs, planes, rows, width = intensity.shape
    x = intensity.reshape(pairs, planes * rows, width)
    scalars = (dir_cos, velocity[None], rate[None], spectrum[None], weight[None])
    parts = main_step(scalars, rough_count, heat, rough_cells[None], rough_map.T, x, n, ns, planes)
    fresh, energy = emit_step(planes, pairs * n, scalars, heat, parts)
    return fresh.reshape(intensity.shape), energy.reshape(planes, rows, width)


def solution(mesh):
    n, ns = mesh.shape["mode"], mesh.shape["space"]
    in_specs = (
        P("mode", None, "space", None),
        P(),
        P(),
        P(),
        P(),
        P(),
        P("space", None),
        P("space"),
        P("space"),
        P("space", None),
    )
    out_specs = (P("mode", None, "space", None), P(None, "space", None))
    return jax.shard_map(
        functools.partial(per_device, n, ns),
        mesh=mesh,
        in_specs=in_specs,
        out_specs=out_specs,
        check_vma=False,
    )
```

```python
import functools

import jax
import jax.numpy as jnp
from jax import lax
from jax.experimental import pallas as pl
from jax.experimental.pallas import tpu as pltpu
from jax.sharding import PartitionSpec as P

MESH = pl.DeviceIdType.MESH
F32 = jnp.float32
BF16 = jnp.bfloat16
SUB, LANE = 8, 128
MIB = 1 << 20


def whole(space=pltpu.VMEM):
    return pl.BlockSpec(memory_space=space)


def in_hbm(*arrays):
    return tuple(pltpu.with_memory_space_constraint(a, pltpu.HBM) for a in arrays)


def squash(energy):
    return energy / (1.0 + 0.3 * jnp.abs(energy))


def send(src, dst, ssem, rsem, axis, target):
    return pltpu.make_async_remote_copy(
        src_ref=src,
        dst_ref=dst,
        send_sem=ssem,
        recv_sem=rsem,
        device_id={axis: target},
        device_id_type=MESH,
    )


class Reduction:
    def __init__(self, acc, slots, part, total, sems, n):
        self.acc, self.slots, self.part, self.total = acc, slots, part, total
        self.sems, self.n = sems, n
        self.me = lax.axis_index("mode")
        self.rows = acc.shape[0] // n

    def chunk(self, i):
        return pl.ds(pl.multiple_of(i * self.rows, self.rows), self.rows)

    def outward(self, off):
        target = lax.rem(self.me + off, self.n)
        return send(
            self.acc.at[self.chunk(target)], self.slots.at[off],
            self.sems.at[0, off], self.sems.at[1, off], "mode", target,
        )

    def spread(self, off):
        target = lax.rem(self.me + off, self.n)
        return send(
            self.part, self.total.at[self.chunk(self.me)],
            self.sems.at[2, off], self.sems.at[3, off], "mode", target,
        )

    def start(self):
        for off in range(1, self.n):
            self.outward(off).start()

    def combine(self, finish):
        for off in range(1, self.n):
            self.outward(off).wait_recv()
        value = self.acc[self.chunk(self.me), :]
        for off in range(1, self.n):
            value = value + self.slots[off]
        self.part[...] = finish(value)
        for off in range(1, self.n):
            self.spread(off).start()
        self.total[self.chunk(self.me), :] = self.part[...]

    def finish(self):
        for off in range(1, self.n):
            source = lax.rem(self.me + self.n - off, self.n)
            send(
                self.part, self.total.at[self.chunk(source)],
                self.sems.at[2, off], self.sems.at[3, off], "mode", source,
            ).wait_recv()
        for off in range(1, self.n):
            self.outward(off).wait_send()
            self.spread(off).wait_send()


def split(value):
    high = value.astype(BF16)
    return high, (value - high.astype(F32)).astype(BF16)


def splat(value):
    return jnp.full((SUB, LANE), value, F32)


def tiles(rows, width):
    return [(r, c) for r in range(0, rows, SUB) for c in range(0, width, LANE)]


def dot(a, b):
    return jnp.dot(a, b, preferred_element_type=F32)


def fine_dot(a, b):
    a_high, a_low = split(a)
    b_high, b_low = split(b)
    return dot(a_high, b_high) + (dot(a_high, b_low) + dot(a_low, b_high))


def turned_dot(a, b):
    contract = (((1,), (1,)), ((), ()))
    high, low = split(a)
    return lax.dot_general(high, b, contract, preferred_element_type=F32) + lax.dot_general(
        low, b, contract, preferred_element_type=F32
    )


def iota(shape, axis):
    return lax.broadcasted_iota(jnp.int32, shape, axis)


def copies(pairs, sem):
    return [pltpu.make_async_copy(src, dst, sem.at[i]) for i, (src, dst) in enumerate(pairs)]


def main_kernel(
    n, ns, planes,
    count, dir_cos_in, velocity_in, rate_in, spectrum_in, weight_in, heat_in, cells_in, reflect_in,
    x,
    xv, returned, glow, equil, summed, smooth, live, marks,
    dir_cos, velocity, rate, spectrum, weight, dir_row, velocity_row, rate_row, spectrum_row,
    weight_row, heat, cells, reflect,
    lo, hi, first, last, acc, slots1, part1, acc2, slots2, part2,
    table, plain, swift, bottom, edge,
    outbox, inbox, wanted, picked, shine, on_row, response, gains,
    psem, lsem, hsem, sems1, sems2, gone, come, back_gone, back_come,
):
    me, sp = lax.axis_index("mode"), lax.axis_index("space")
    pairs, total_rows, width = xv.shape
    rows = total_rows // planes
    modes = velocity.shape[1]
    dirs = pairs // modes
    half = dirs // 2
    quiet = half * modes
    ups = reflect.shape[0]
    pairs_total = pairs * n
    rough = cells.shape[1]
    share = rough // n
    piece = quiet // 4
    batch = min(16, modes)
    per_dir = modes // batch
    order = [d for d in range(1, dirs, 2)] + [d for d in range(0, dirs, 2)]
    chunks = [(d, b) for d in order for b in range(per_dir)]

    fetched = copies((
        (cells_in, cells), (weight_in, weight), (dir_cos_in, dir_cos), (velocity_in, velocity),
        (rate_in, rate), (spectrum_in, spectrum), (dir_cos_in, dir_row),
        (velocity_in, velocity_row), (rate_in, rate_row), (spectrum_in, spectrum_row),
        (weight_in, weight_row), (heat_in, heat), (reflect_in, reflect),
    ), psem)
    for copy in fetched:
        copy.start()

    def load(i):
        d, b = chunks[i]
        where = pl.ds(d * modes + b * batch, batch)
        return pltpu.make_async_copy(x.at[where], xv.at[where], lsem.at[i])

    for i in range(len(chunks)):
        load(i).start()

    barrier = pltpu.get_barrier_semaphore()
    for off in range(1, n):
        pl.semaphore_signal(
            barrier, inc=1, device_id={"mode": lax.rem(me + off, n)}, device_id_type=MESH
        )

    @pl.when(sp > 0)
    def _():
        pl.semaphore_signal(barrier, inc=1, device_id={"space": sp - 1}, device_id_type=MESH)

    @pl.when(sp < ns - 1)
    def _():
        pl.semaphore_signal(barrier, inc=1, device_id={"space": sp + 1}, device_id_type=MESH)

    @pl.when(sp == 0)
    def _():
        lo[...] = jnp.zeros_like(lo)

    @pl.when(sp == ns - 1)
    def _():
        hi[...] = jnp.zeros_like(hi)

    acc[...] = jnp.zeros_like(acc)
    acc2[...] = jnp.zeros_like(acc2)
    for copy in fetched:
        copy.wait()
    marks[...] = jnp.where(iota((width, rough), 0) == lax.rem(cells[...], width), 1.0, 0.0).astype(
        BF16
    )
    on_row[...] = jnp.where(iota((rows, rough), 0) == cells[...] // width, 1.0, 0.0)
    low = jnp.where(sp > 0, 1, 0)
    high = jnp.where(sp < ns - 1, 1, 0)
    pl.semaphore_wait(barrier, n - 1 + low + high)

    def down_copy(i):
        d, b = chunks[i]
        where = pl.ds(d * modes + b * batch, batch)
        return send(
            first.at[:, :, where], hi.at[:, :, where], hsem.at[0, i], hsem.at[1, i], "space",
            lax.rem(sp + ns - 1, ns),
        )

    def up_copy(i):
        d, b = chunks[i]
        where = pl.ds(d * modes + b * batch, batch)
        return send(
            last.at[:, :, where], lo.at[:, :, where], hsem.at[2, i], hsem.at[3, i], "space",
            lax.rem(sp + 1, ns),
        )

    def halo_wait(i):
        @pl.when(sp > 0)
        def _():
            down_copy(i).wait_send()
            up_copy(i).wait_recv()

        @pl.when(sp < ns - 1)
        def _():
            up_copy(i).wait_send()
            down_copy(i).wait_recv()

    def take(i):
        d, b = chunks[i]
        base = d * modes + b * batch
        load(i).wait()

        def edges(t, carry):
            p = base + t
            for z in range(planes):
                for k in range(width // LANE):
                    cols = pl.ds(k * LANE, LANE)
                    first[k, z, pl.ds(p, 1), :] = xv[p, pl.ds(z * rows, 1), cols]
                    last[k, z, pl.ds(p, 1), :] = xv[p, pl.ds((z + 1) * rows - 1, 1), cols]
            return carry

        lax.fori_loop(0, batch, edges, 0)

        @pl.when(sp > 0)
        def _():
            down_copy(i).start()

        @pl.when(sp < ns - 1)
        def _():
            up_copy(i).start()

        survey(d, b * batch, b * batch + batch)

    row, lane = iota((SUB, LANE), 0), iota((SUB, LANE), 1)
    places = tiles(rows, width)
    last_row, last_col = rows - SUB, width - LANE

    def gain(d, kind, m):
        return jnp.broadcast_to(table[d, kind, pl.ds(m, 1), :], (SUB, LANE))

    def cosines(d):
        return [jnp.abs(dir_cos[axis, me * dirs + d]) for axis in range(3)]

    def signs(d):
        s = me * dirs + d
        low_x, low_y = splat(dir_cos[0, s]) >= 0.0, splat(dir_cos[1, s]) >= 0.0
        return (
            jnp.where(dir_cos[0, s] >= 0.0, 1, SUB - 1),
            jnp.where(dir_cos[1, s] >= 0.0, 1, LANE - 1),
            low_x & (row == 0), ~low_x & (row == SUB - 1),
            low_y & (lane == 0), ~low_y & (lane == LANE - 1),
        )

    def level_order(d):
        return list(range(planes)) if d % 2 == 0 else list(reversed(range(planes)))

    def tabulate():
        same = iota((modes, modes), 0) == iota((modes, modes), 1)

        def column(values):
            return jnp.sum(jnp.where(same, values, 0.0), axis=1, keepdims=True)

        v, e, f = column(velocity_row[...]), column(rate_row[...]), column(spectrum_row[...])
        for d in range(dirs):
            inv = 1.0 / (1.0 + e + v * cosines(d)[2])
            for kind, value in enumerate((inv, inv * v, inv * (e * f))):
                table[d, kind] = jnp.broadcast_to(value, (modes, LANE))

    def survey(d, start, stop):
        cz = cosines(d)[2]
        w = weight[0, me * dirs + d]
        levels = level_order(d)
        for r, c in places:
            cols = pl.ds(c, LANE)

            def one(t, carry):
                sums = [list(part) for part in carry]
                for m in (start + 2 * t, start + 2 * t + 1):
                    inv, fast = gain(d, 0, m), gain(d, 1, m)
                    kp = fast * cz
                    u = None
                    for z in levels:
                        value = xv[d * modes + m, pl.ds(z * rows + r, SUB), cols]
                        u = value if u is None else value + kp * u
                        sums[0][z] = sums[0][z] + value
                        sums[1][z] = sums[1][z] + inv * u
                        sums[2][z] = sums[2][z] + fast * u
                    if d % 2:
                        bottom[d // 2 * modes + m, pl.ds(r, SUB), cols] = u
                return tuple(tuple(part) for part in sums)

            zero = tuple(jnp.zeros((SUB, LANE), F32) for _ in range(planes))
            sums = lax.fori_loop(0, (stop - start) // 2, one, (zero, zero, zero))
            for z in range(planes):
                here = pl.ds(z * rows + r, SUB)
                acc[here, cols] += w * sums[0][z]
                if start == 0:
                    plain[d, here, cols] = sums[1][z]
                    swift[d, here, cols] = sums[2][z]
                else:
                    plain[d, here, cols] += sums[1][z]
                    swift[d, here, cols] += sums[2][z]

    def neighbours(own, kinds):
        shift_x, shift_y, head_x, tail_x, head_y, tail_y = kinds
        side = {at: pltpu.roll(own[at], shift_x, 0) for at in places}
        along = {at: pltpu.roll(own[at], shift_y, 1) for at in places}
        ones, twos = {}, {}
        for r, c in places:
            under = side[r - SUB, c] if r else 0.0
            over = side[r + SUB, c] if r < last_row else 0.0
            ones[r, c] = jnp.where(head_x, under, jnp.where(tail_x, over, side[r, c]))
            left = along[r, c - LANE] if c else 0.0
            right = along[r, c + LANE] if c < last_col else 0.0
            twos[r, c] = jnp.where(head_y, left, jnp.where(tail_y, right, along[r, c]))
        return ones, twos

    def edge_rows(d):
        s = me * dirs + d
        w = weight[0, s]
        cx, _, cz = cosines(d)
        _, _, head_x, tail_x, _, _ = signs(d)
        from_low = splat(dir_cos[0, s]) >= 0.0
        for c in range(0, width, LANE):
            cols = pl.ds(c, LANE)
            totals = [None] * planes
            for m in range(0, modes, SUB):
                fast = table[d, 1, pl.ds(m, SUB), :]
                kp, kx = fast * cz, fast * cx
                here = pl.ds(d * modes + m, SUB)
                u = None
                for z in level_order(d):
                    value = jnp.where(from_low, lo[c // LANE, z, here], hi[c // LANE, z, here])
                    u = value if u is None else value + kp * u
                    now = kx * u
                    totals[z] = now if totals[z] is None else totals[z] + now
                if d % 2:
                    edge[c // LANE, pl.ds(d // 2 * modes + m, SUB), :] = now
            for z in range(planes):
                line = jnp.broadcast_to(jnp.sum(totals[z], axis=0, keepdims=True), (SUB, LANE))
                top, end = pl.ds(z * rows, SUB), pl.ds(z * rows + last_row, SUB)
                acc2[top, cols] += jnp.where(head_x, w * line, 0.0)
                acc2[end, cols] += jnp.where(tail_x, w * line, 0.0)

    def ground(start, stop):
        d = 2 * (start // modes) + 1
        cx, cy, _ = cosines(d)
        kinds = signs(d)
        head_x, tail_x = kinds[2:4]

        def one(t, carry):
            q = start + t
            m = start % modes + t
            inv, fast = gain(d, 0, m), gain(d, 1, m)
            kx, ky = fast * cx, fast * cy
            k0 = inv - kx - ky
            own = {(r, c): bottom[q, pl.ds(r, SUB), pl.ds(c, LANE)] for r, c in places}
            ones, twos = neighbours(own, kinds)
            for r, c in places:
                value = k0 * own[r, c] + kx * ones[r, c] + ky * twos[r, c]
                line = jnp.broadcast_to(edge[c // LANE, pl.ds(q, 1), :], (SUB, LANE))
                if r == 0:
                    value = value + jnp.where(head_x, line, 0.0)
                if r == last_row:
                    value = value + jnp.where(tail_x, line, 0.0)
                bottom[q, pl.ds(r, SUB), pl.ds(c, LANE)] = value
            return carry

        lax.fori_loop(0, stop - start, one, 0)

    def glide(h):
        cz = cosines(2 * h)[2]
        w = weight[0, me * dirs + 2 * h]
        for r, c in places:
            cols = pl.ds(c, LANE)

            def one(t, carry):
                sums = list(carry)
                for m in (2 * t, 2 * t + 1):
                    kp = gain(2 * h, 1, m) * cz
                    value = bottom[h * modes + m, pl.ds(r, SUB), cols]
                    for z in range(planes):
                        value = kp * value
                        sums[z] = sums[z] + value
                return tuple(sums)

            zero = tuple(jnp.zeros((SUB, LANE), F32) for _ in range(planes))
            sums = lax.fori_loop(0, modes // 2, one, zero)
            scale = w * smooth[pl.ds(r, SUB), cols]
            for z in range(planes):
                acc2[pl.ds(z * rows + r, SUB), cols] += scale * sums[z]

    def tally(d):
        cx, cy, _ = cosines(d)
        w = weight[0, me * dirs + d]
        kinds = signs(d)

        def one(z, carry):
            at = {
                (r, c): (pl.ds(pl.multiple_of(z * rows, SUB) + r, SUB), pl.ds(c, LANE))
                for r, c in places
            }
            own = {k: swift[(d, *at[k])] for k in places}
            ones, twos = neighbours(own, kinds)
            for k in places:
                value = plain[(d, *at[k])] - (cx + cy) * own[k] + cx * ones[k] + cy * twos[k]
                acc2[at[k]] += w * value
            return carry

        lax.fori_loop(0, planes, one, 0)

    halo_done = set()

    def halo_for(d, start, stop):
        for i, (dd, b) in enumerate(chunks):
            if dd == d and b * batch < stop and start < (b + 1) * batch and i not in halo_done:
                halo_done.add(i)
                halo_wait(i)

    def sweep(d, start, stop):
        halo_for(d, start, stop)
        cx, cy, cz = cosines(d)
        shift_x, shift_y, head_x, tail_x, head_y, tail_y = signs(d)
        wide = 2

        def some(g, carry):
            sets, before = [], []
            for t in range(wide):
                m = start + g * wide + t
                inv, fast = gain(d, 0, m), gain(d, 1, m)
                kx, ky = fast * cx, fast * cy
                sets.append((
                    d * modes + m, inv - kx - ky, kx, fast * cz,
                    ky, jnp.where(head_y, 0.0, ky), jnp.where(tail_y, 0.0, ky),
                ))
                if d % 2 == 0:
                    before.append({
                        (r, c): smooth[pl.ds(r, SUB), pl.ds(c, LANE)]
                        * bottom[d // 2 * modes + m, pl.ds(r, SUB), pl.ds(c, LANE)]
                        for r, c in places
                    })
                else:
                    before.append(None)
            for z in range(planes) if d % 2 == 0 else reversed(range(planes)):
                for t in range(wide):
                    p, k0, kx, kp, ky, ky_head, ky_tail = sets[t]
                    own = {
                        (r, c): xv[p, pl.ds(z * rows + r, SUB), pl.ds(c, LANE)] for r, c in places
                    }
                    side = {at: pltpu.roll(own[at], shift_x, 0) for at in places}
                    along = {at: pltpu.roll(own[at], shift_y, 1) for at in places}
                    now = {}
                    for r, c in places:
                        cols = pl.ds(c, LANE)
                        if r == 0:
                            under = jnp.broadcast_to(lo[c // LANE, z, pl.ds(p, 1), :], (SUB, LANE))
                        else:
                            under = side[r - SUB, c]
                        if r == last_row:
                            over = jnp.broadcast_to(hi[c // LANE, z, pl.ds(p, 1), :], (SUB, LANE))
                        else:
                            over = side[r + SUB, c]
                        one = jnp.where(head_x, under, jnp.where(tail_x, over, side[r, c]))
                        two = along[r, c]
                        if c > 0:
                            two = jnp.where(head_y, along[r, c - LANE], two)
                        if c < last_col:
                            two = jnp.where(tail_y, along[r, c + LANE], two)
                        weigh = ky
                        if c == 0:
                            weigh = ky_head
                        if c == last_col:
                            weigh = ky_tail if c else jnp.where(tail_y, 0.0, ky_head)
                        value = k0 * own[r, c] + kx * one + weigh * two
                        if before[t] is not None:
                            value = value + kp * before[t][r, c]
                        now[r, c] = value
                        xv[p, pl.ds(z * rows + r, SUB), cols] = value
                    before[t] = now
            return carry

        lax.fori_loop(0, (stop - start) // wide, some, 0)

    def settle(h, start, stop):
        wide = 2
        up, down = 2 * h, 2 * h + 1

        def some(g, carry):
            sets, values = [], []
            for t in range(wide):
                m = start + g * wide + t
                sets.append((m, gain(up, 1, m) * cosines(up)[2], gain(up, 2, m)))
                values.append({
                    (r, c): heat[pl.ds(r, SUB), pl.ds(c, LANE)] * spectrum[0, m] for r, c in places
                })
            for d, z in [(down, z) for z in reversed(range(planes))] + [
                (up, z) for z in range(planes)
            ]:
                for r, c in places:
                    here, cols = pl.ds(z * rows + r, SUB), pl.ds(c, LANE)
                    level = equil[here, cols]
                    for t in range(wide):
                        m, kp, ks = sets[t]
                        value = values[t][r, c]
                        if d == up and z == 0:
                            value = value * smooth[pl.ds(r, SUB), cols]
                        value = kp * value + ks * level
                        values[t][r, c] = value
                        xv[d * modes + m, here, cols] += value
            return carry

        lax.fori_loop(0, (stop - start) // wide, some, 0)

    def at_slots(values):
        k = values.shape[0]
        high, low = split(values.reshape(k * rows, width))
        column = marks[...]
        got = dot(high, column) + dot(low, column)
        return jnp.sum(got.reshape(k, rows, rough) * on_row[...][None], axis=1)

    def shares(values):
        return [values[:, i * share : (i + 1) * share] for i in range(n)]

    def outward(part, off):
        target = lax.rem(me + off, n)
        here = pl.ds(part * piece, piece)
        return send(
            outbox.at[target, here], inbox.at[me, here], gone.at[part, off], come.at[part, off],
            "mode", target,
        )

    def arrival(part, off):
        source = lax.rem(me + n - off, n)
        here = pl.ds(part * piece, piece)
        return send(
            outbox.at[source, here], inbox.at[source, here], gone.at[part, off],
            come.at[part, off], "mode", source,
        )

    def homeward(off):
        target = lax.rem(me + off, n)
        mine = pl.ds(pl.multiple_of(target * quiet, quiet), quiet)
        return [
            send(
                picked.at[mine], returned.at[me], back_gone.at[0, off], back_come.at[0, off],
                "mode", target,
            ),
            send(shine, glow.at[me], back_gone.at[1, off], back_come.at[1, off], "mode", target),
        ]

    def return_of(off):
        source = lax.rem(me + n - off, n)
        mine = pl.ds(pl.multiple_of(me * quiet, quiet), quiet)
        return [
            send(
                picked.at[mine], returned.at[source], back_gone.at[0, off], back_come.at[0, off],
                "mode", source,
            ),
            send(
                shine, glow.at[source], back_gone.at[1, off], back_come.at[1, off], "mode", source
            ),
        ]

    def launch(part):
        q = part * piece
        ground(q, q + piece)
        got = at_slots(bottom[pl.ds(q, piece)])
        for i, value in enumerate(shares(got)):
            outbox[i, pl.ds(q, piece), :] = value
        for off in range(1, n):
            outward(part, off).start()
        inbox[me, pl.ds(q, piece), :] = outbox[me, pl.ds(q, piece), :]

    def own_share(values):
        total = jnp.zeros((values.shape[0], share), values.dtype)
        for i, value in enumerate(shares(values)):
            total = jnp.where(me == i, value, total)
        return total

    def choose():
        for part in range(4):
            for off in range(1, n):
                arrival(part, off).wait_recv()
        lanes = response.shape[1]
        levels = at_slots(equil[...].reshape(planes, rows, width))
        face = at_slots(heat[...].reshape(1, rows, width))
        spare = jnp.zeros((lanes - planes - 1, rough), F32)
        sources = own_share(jnp.concatenate([levels, face, spare], axis=0))
        lift = fine_dot(response[...], sources)
        inbox[...] += lift.reshape(n, quiet, share)
        wanted[...] = own_share(reflect[...])

        def one(k, carry):
            want = wanted[pl.ds(k, 1), :]
            value = None
            for j in range(ups):
                source = inbox[j // half, pl.ds((j % half) * modes, modes), :]
                value = source if j == 0 else jnp.where(want == j, source, value)
            picked[pl.ds(pl.multiple_of(k * modes, modes), modes), :] = value
            return carry

        lax.fori_loop(0, ups, one, 0)
        shine[...] = fine_dot(gains[...], picked[...])
        for off in range(1, n):
            for copy in homeward(off):
                copy.start()
        returned[me] = picked[pl.ds(pl.multiple_of(me * quiet, quiet), quiet), :]
        glow[me] = shine[...]

    def prepare():
        size, lanes = ups * modes, response.shape[1]
        which = iota((size, 1), 0)
        modal = iota((size, modes), 1) == lax.rem(which, modes)
        angle = iota((size, 2 * ups), 1) == 2 * (which // modes) + 1

        def spread(mask, values):
            return jnp.sum(jnp.where(mask, values, 0.0), axis=1, keepdims=True)

        v, e = spread(modal, velocity_row[...]), spread(modal, rate_row[...])
        f = spread(modal, spectrum_row[...])
        turn = v * spread(angle, jnp.abs(dir_row[pl.ds(2, 1), :]))
        inv = 1.0 / (1.0 + e + turn)
        kp, power = turn * inv, inv * (e * f)
        at = iota((size, lanes), 1)
        out = jnp.zeros((size, lanes), F32)
        for z in range(planes):
            out = jnp.where(at == z, power, out)
            power = power * kp
        power = f * kp
        for z in range(planes - 1):
            power = power * kp
        response[...] = jnp.where(at == planes, power, out)

        which = iota((1, size), 1)

        def along(values, index):
            length = values.shape[1]
            same = iota((length, length), 0) == iota((length, length), 1)
            column = jnp.sum(jnp.where(same, values, 0.0), axis=1, keepdims=True)
            mask = iota((length, size), 0) == index
            return jnp.sum(jnp.where(mask, column, 0.0), axis=0, keepdims=True)

        modal, angle = lax.rem(which, modes), 2 * (which // modes)
        v, e = along(velocity_row[...], modal), along(rate_row[...], modal)
        turn = v * along(jnp.abs(dir_row[pl.ds(2, 1), :]), angle)
        kp = turn / (1.0 + e + turn)
        power = 0.9 * along(weight_row[...], angle)
        for z in range(planes):
            power = power * kp
            gains[pl.ds(z, 1), :] = power

    def find_rough():
        live[...] = jnp.where(iota((rows, rough), 1) < count[0], on_row[...], 0.0)
        rough_at = lax.dot_general(
            live[...].astype(BF16), marks[...], (((1,), (1,)), ((), ())), preferred_element_type=F32
        )
        smooth[...] = jnp.where(rough_at > 0.5, 0.0, 0.9)

    opening = Reduction(acc, slots1, part1, equil, sems1, n)
    closing = Reduction(acc2, slots2, part2, summed, sems2, n)

    tabulate()
    for i in range(len(chunks)):
        take(i)
    opening.start()
    for d in range(1, dirs, 2):
        halo_for(d, 0, modes)
        edge_rows(d)
    for part in range(4):
        launch(part)
    find_rough()
    opening.combine(lambda value: squash(value * (1.0 / pairs_total)))
    for h in range(half):
        glide(h)
    for d in range(dirs):
        tally(d)
    for d in range(0, dirs, 2):
        halo_for(d, 0, modes)
        edge_rows(d)
    closing.start()
    prepare()
    slices = [(d, m) for d in range(dirs) for m in range(0, modes, SUB)]
    cuts = [len(slices) * i // 8 for i in (0, 2, 5, 8)]
    for d, m in slices[cuts[0] : cuts[1]]:
        sweep(d, m, m + SUB)
    opening.finish()
    choose()
    for d, m in slices[cuts[1] : cuts[2]]:
        sweep(d, m, m + SUB)
    closing.combine(lambda value: value)
    for d, m in slices[cuts[2] : cuts[3]]:
        sweep(d, m, m + SUB)
    for h in range(half):
        settle(h, 0, modes)
    closing.finish()
    for off in range(1, n):
        for copy in return_of(off):
            copy.wait_recv()
    for off in range(1, n):
        for part in range(4):
            outward(part, off).wait_send()
        for copy in homeward(off):
            copy.wait_send()


def main_step(scalars, count, heat, cells, reflect, x, n, ns, planes):
    pairs, total_rows, width = x.shape
    rows = total_rows // planes
    modes = scalars[1].shape[1]
    quiet = pairs // 2
    rough = cells.shape[1]
    every = reflect.shape[0] * modes
    share = rough // n
    n_chunks = (pairs // modes) * (modes // min(16, modes))
    flat = (total_rows, width)
    part = (total_rows // n, width)
    halo = pltpu.VMEM((width // LANE, planes, pairs, LANE), F32)
    lanes = -(-(planes + 1) // 16) * 16
    return pl.pallas_call(
        functools.partial(main_kernel, n, ns, planes),
        out_shape=(
            jax.ShapeDtypeStruct(x.shape, F32),
            jax.ShapeDtypeStruct((n, quiet, share), F32),
            jax.ShapeDtypeStruct((n, planes, share), F32),
            jax.ShapeDtypeStruct(flat, F32),
            jax.ShapeDtypeStruct(flat, F32),
            jax.ShapeDtypeStruct((rows, width), F32),
            jax.ShapeDtypeStruct((rows, rough), F32),
            jax.ShapeDtypeStruct((width, rough), BF16),
        ),
        in_specs=[whole(pltpu.SMEM)] + [whole(pltpu.HBM)] * 9,
        out_specs=(whole(),) * 8,
        scratch_shapes=[
            *(pltpu.SMEM(a.shape, a.dtype) for a in scalars),
            *(pltpu.VMEM(a.shape, a.dtype) for a in (*scalars, heat, cells, reflect)),
            halo, halo, halo, halo,
            pltpu.VMEM(flat, F32),
            pltpu.VMEM((n, *part), F32),
            pltpu.VMEM(part, F32),
            pltpu.VMEM(flat, F32),
            pltpu.VMEM((n, *part), F32),
            pltpu.VMEM(part, F32),
            pltpu.VMEM((pairs // modes, 3, modes, LANE), F32),
            pltpu.VMEM((pairs // modes, *flat), F32),
            pltpu.VMEM((pairs // modes, *flat), F32),
            pltpu.VMEM((quiet, rows, width), F32),
            pltpu.VMEM((width // LANE, quiet, LANE), F32),
            pltpu.VMEM((n, quiet, share), F32),
            pltpu.VMEM((n, quiet, share), F32),
            pltpu.VMEM((reflect.shape[0], share), jnp.int32),
            pltpu.VMEM((every, share), F32),
            pltpu.VMEM((planes, share), F32),
            pltpu.VMEM((rows, rough), F32),
            pltpu.VMEM((every, lanes), F32),
            pltpu.VMEM((planes, every), F32),
            pltpu.SemaphoreType.DMA((13,)),
            pltpu.SemaphoreType.DMA((n_chunks,)),
            pltpu.SemaphoreType.DMA((4, n_chunks)),
            pltpu.SemaphoreType.DMA((4, n)),
            pltpu.SemaphoreType.DMA((4, n)),
            pltpu.SemaphoreType.DMA((4, n)),
            pltpu.SemaphoreType.DMA((4, n)),
            pltpu.SemaphoreType.DMA((2, n)),
            pltpu.SemaphoreType.DMA((2, n)),
        ],
        compiler_params=pltpu.CompilerParams(
            collective_id=0, has_side_effects=True, vmem_limit_bytes=28 * MIB
        ),
        name="main_step",
    )(count, *in_hbm(*scalars, heat, cells, reflect, x))


def emit_kernel(
    planes, pairs_total, dir_cos_in, velocity_in, rate_in, spectrum_in, weight_in, heat_in,
    xv, returned, glow, equil, summed, smooth, live, marks,
    out, energy,
    dir_cos, velocity, rate, dir_row, velocity_row, rate_row, spectrum_row, weight_row, heat,
    rising, inflow, moments, psem, sem,
):
    pairs, total_rows, width = xv.shape
    rows = total_rows // planes
    modes = velocity.shape[1]
    dirs = pairs // modes
    half = dirs // 2
    rough = live.shape[1]
    n = returned.shape[0]
    every = n * half * modes
    batch = min(8, modes)
    me = lax.axis_index("mode")
    places = tiles(rows, width)

    def whole_dir(d):
        where = pl.ds(d * modes, modes)
        return pltpu.make_async_copy(xv.at[where], out.at[where], sem.at[d, 0])

    def piece(d, b):
        return pltpu.make_async_copy(
            rising.at[pl.ds(d // 2 * modes + b * batch, batch)],
            out.at[pl.ds(d * modes + b * batch, batch)], sem.at[d, b],
        )

    fetched = copies((
        (dir_cos_in, dir_cos), (velocity_in, velocity), (rate_in, rate), (dir_cos_in, dir_row),
        (velocity_in, velocity_row), (rate_in, rate_row), (spectrum_in, spectrum_row),
        (weight_in, weight_row), (heat_in, heat),
    ), psem)
    for copy in fetched:
        copy.start()
    for d in range(1, dirs, 2):
        whole_dir(d).start()
    for copy in fetched:
        copy.wait()

    group = min(16, modes)
    for d in range(0, dirs, 2):
        cz = jnp.abs(dir_cos[2, me * dirs + d])
        for g in range(modes // group):
            first = pl.ds(d // 2 * modes + g * group, group)
            own = jnp.concatenate([returned[i, first, :] for i in range(n)], axis=1)
            spread = own[:, None, :] * live[...][None]
            put = turned_dot(spread.reshape(group * rows, rough), marks[...])
            inflow[...] = 0.9 * put.reshape(group, rows, width)
            for b in range(g * group // batch, (g + 1) * group // batch):
                def one(i, carry):
                    m = b * batch + i
                    turn = velocity[0, m] * cz
                    ratio = splat(turn) / splat(1.0 + rate[0, m] + turn)
                    for r, c in places:
                        cols = pl.ds(c, LANE)
                        value = inflow[m - g * group, pl.ds(r, SUB), cols]
                        for z in range(planes):
                            here = pl.ds(z * rows + r, SUB)
                            value = ratio * value
                            rising[d // 2 * modes + m, here, cols] = (
                                xv[d * modes + m, here, cols] + value
                            )
                    return carry

                lax.fori_loop(0, batch, one, 0)
                piece(d, b).start()

    n_dirs = weight_row.shape[1]

    def column(values):
        size = values.shape[1]
        same = iota((size, size), 0) == iota((size, size), 1)
        return jnp.sum(jnp.where(same, values, 0.0), axis=1, keepdims=True)

    which = iota((1, every), 1)

    def spread_over(values, index):
        size = values.shape[1]
        mask = iota((size, every), 0) == index
        return jnp.sum(jnp.where(mask, column(values), 0.0), axis=0, keepdims=True)

    modal, angle = lax.rem(which, modes), 2 * (which // modes)
    v, e = spread_over(velocity_row[...], modal), spread_over(rate_row[...], modal)
    f = spread_over(spectrum_row[...], modal)
    turn = v * spread_over(jnp.abs(dir_row[pl.ds(2, 1), :]), angle)
    w_up, w_down = spread_over(weight_row[...], angle), spread_over(weight_row[...], angle + 1)
    inv = 1.0 / (1.0 + e + turn)
    kp, ks = turn * inv, inv * (e * f)
    top = 2 * planes + 2
    power = jnp.ones_like(kp)
    for q in range(top):
        for i, scale in enumerate((w_up * ks, w_down * ks, w_up * f, w_down * f)):
            total = jnp.sum(scale * power, axis=1, keepdims=True)
            moments[i, pl.ds(q, 1), :] = jnp.broadcast_to(total, (1, LANE))
        power = power * kp
    at_slot = jnp.concatenate([glow[i] for i in range(n)], axis=1)
    spread = at_slot[:, None, :] * live[...][None]
    rough_part = turned_dot(spread.reshape(total_rows, rough), marks[...])

    def moment(i, q):
        return jnp.broadcast_to(moments[i, pl.ds(q, 1), :], (SUB, LANE))

    for r, c in places:
        cols = pl.ds(c, LANE)
        levels = [equil[pl.ds(z * rows + r, SUB), cols] for z in range(planes)]
        face = heat[pl.ds(r, SUB), cols]
        plain = smooth[pl.ds(r, SUB), cols]
        for z in range(planes):
            here = pl.ds(z * rows + r, SUB)
            value = summed[here, cols] + rough_part[z * rows + r : z * rows + r + SUB, c : c + LANE]
            value = value + moment(3, planes - z) * face
            turned = moment(2, z + 1 + planes) * face
            for y in range(planes):
                if y <= z:
                    value = value + moment(0, z - y) * levels[y]
                if y >= z:
                    value = value + moment(1, y - z) * levels[y]
                turned = turned + moment(0, z + 1 + y) * levels[y]
            energy[here, cols] = (value + plain * turned) * (1.0 / pairs_total)
    for d in range(dirs):
        if d % 2:
            whole_dir(d).wait()
        else:
            for b in range(modes // batch):
                piece(d, b).wait()


def emit_step(planes, pairs_total, scalars, heat, parts):
    xv = parts[0]
    pairs, total_rows, width = xv.shape
    modes = scalars[1].shape[1]
    rows = total_rows // planes
    return pl.pallas_call(
        functools.partial(emit_kernel, planes, pairs_total),
        out_shape=(
            jax.ShapeDtypeStruct(xv.shape, F32),
            jax.ShapeDtypeStruct((total_rows, width), F32),
        ),
        in_specs=[whole(pltpu.HBM)] * 6 + [whole()] * len(parts),
        out_specs=(whole(pltpu.HBM), whole()),
        scratch_shapes=[
            *(pltpu.SMEM(a.shape, a.dtype) for a in scalars[:3]),
            *(pltpu.VMEM(a.shape, a.dtype) for a in (*scalars, heat)),
            pltpu.VMEM((pairs // 2, total_rows, width), F32),
            pltpu.VMEM((min(16, modes), rows, width), F32),
            pltpu.VMEM((4, -(-(2 * planes + 2) // SUB) * SUB, LANE), F32),
            pltpu.SemaphoreType.DMA((9,)),
            pltpu.SemaphoreType.DMA((pairs // modes, modes // min(8, modes))),
        ],
        compiler_params=pltpu.CompilerParams(vmem_limit_bytes=28 * MIB),
        name="emit_step",
    )(*in_hbm(*scalars, heat), *parts)


def per_device(
    n, ns, intensity, dir_cos, velocity, rate, spectrum, weight, heat, rough_cells, rough_count,
    rough_map,
):
    pairs, planes, rows, width = intensity.shape
    x = intensity.reshape(pairs, planes * rows, width)
    scalars = (dir_cos, velocity[None], rate[None], spectrum[None], weight[None])
    parts = main_step(scalars, rough_count, heat, rough_cells[None], rough_map.T, x, n, ns, planes)
    fresh, energy = emit_step(planes, pairs * n, scalars, heat, parts)
    return fresh.reshape(intensity.shape), energy.reshape(planes, rows, width)


def solution(mesh):
    n, ns = mesh.shape["mode"], mesh.shape["space"]
    in_specs = (
        P("mode", None, "space", None),
        P(),
        P(),
        P(),
        P(),
        P(),
        P("space", None),
        P("space"),
        P("space"),
        P("space", None),
    )
    out_specs = (P("mode", None, "space", None), P(None, "space", None))
    return jax.shard_map(
        functools.partial(per_device, n, ns),
        mesh=mesh,
        in_specs=in_specs,
        out_specs=out_specs,
        check_vma=False,
    )
```

```python
import functools

import jax
import jax.numpy as jnp
from jax import lax
from jax.experimental import pallas as pl
from jax.experimental.pallas import tpu as pltpu
from jax.sharding import PartitionSpec as P

MESH = pl.DeviceIdType.MESH
F32 = jnp.float32
BF16 = jnp.bfloat16
SUB, LANE = 8, 128
MIB = 1 << 20


def whole(space=pltpu.VMEM):
    return pl.BlockSpec(memory_space=space)


def in_hbm(*arrays):
    return tuple(pltpu.with_memory_space_constraint(a, pltpu.HBM) for a in arrays)


def squash(energy):
    return energy / (1.0 + 0.3 * jnp.abs(energy))


def send(src, dst, ssem, rsem, axis, target):
    return pltpu.make_async_remote_copy(
        src_ref=src,
        dst_ref=dst,
        send_sem=ssem,
        recv_sem=rsem,
        device_id={axis: target},
        device_id_type=MESH,
    )


class Reduction:
    def __init__(self, acc, slots, part, total, sems, n):
        self.acc, self.slots, self.part, self.total = acc, slots, part, total
        self.sems, self.n = sems, n
        self.me = lax.axis_index("mode")
        self.rows = acc.shape[0] // n

    def chunk(self, i):
        return pl.ds(pl.multiple_of(i * self.rows, self.rows), self.rows)

    def outward(self, off):
        target = lax.rem(self.me + off, self.n)
        return send(
            self.acc.at[self.chunk(target)], self.slots.at[off],
            self.sems.at[0, off], self.sems.at[1, off], "mode", target,
        )

    def spread(self, off):
        target = lax.rem(self.me + off, self.n)
        return send(
            self.part, self.total.at[self.chunk(self.me)],
            self.sems.at[2, off], self.sems.at[3, off], "mode", target,
        )

    def start(self):
        for off in range(1, self.n):
            self.outward(off).start()

    def combine(self, finish):
        for off in range(1, self.n):
            self.outward(off).wait_recv()
        value = self.acc[self.chunk(self.me), :]
        for off in range(1, self.n):
            value = value + self.slots[off]
        self.part[...] = finish(value)
        for off in range(1, self.n):
            self.spread(off).start()
        self.total[self.chunk(self.me), :] = self.part[...]

    def finish(self):
        for off in range(1, self.n):
            source = lax.rem(self.me + self.n - off, self.n)
            send(
                self.part, self.total.at[self.chunk(source)],
                self.sems.at[2, off], self.sems.at[3, off], "mode", source,
            ).wait_recv()
        for off in range(1, self.n):
            self.outward(off).wait_send()
            self.spread(off).wait_send()


def split(value):
    high = value.astype(BF16)
    return high, (value - high.astype(F32)).astype(BF16)


def splat(value):
    return jnp.full((SUB, LANE), value, F32)


def tiles(rows, width):
    return [(r, c) for r in range(0, rows, SUB) for c in range(0, width, LANE)]


def dot(a, b):
    return jnp.dot(a, b, preferred_element_type=F32)


def fine_dot(a, b):
    a_high, a_low = split(a)
    b_high, b_low = split(b)
    return dot(a_high, b_high) + (dot(a_high, b_low) + dot(a_low, b_high))


def turned_dot(a, b):
    contract = (((1,), (1,)), ((), ()))
    high, low = split(a)
    return lax.dot_general(high, b, contract, preferred_element_type=F32) + lax.dot_general(
        low, b, contract, preferred_element_type=F32
    )


def iota(shape, axis):
    return lax.broadcasted_iota(jnp.int32, shape, axis)


def copies(pairs, sem):
    return [pltpu.make_async_copy(src, dst, sem.at[i]) for i, (src, dst) in enumerate(pairs)]


def main_kernel(
    n, ns, planes,
    count, dir_cos_in, velocity_in, rate_in, spectrum_in, weight_in, heat_in, cells_in, reflect_in,
    x,
    xv, returned, glow, equil, summed, smooth, live, marks,
    dir_cos, velocity, rate, spectrum, weight, dir_row, velocity_row, rate_row, spectrum_row,
    weight_row, heat, cells, reflect,
    lo, hi, first, last, acc, slots1, part1, acc2, slots2, part2,
    table, outbox, inbox, wanted, picked, shine, on_row, response, gains,
    psem, lsem, hsem, sems1, sems2, gone, come, back_gone, back_come,
):
    me, sp = lax.axis_index("mode"), lax.axis_index("space")
    pairs, strips, total_rows, _ = xv.shape
    width = strips * LANE
    rows = total_rows // planes
    modes = velocity.shape[1]
    dirs = pairs // modes
    half = dirs // 2
    quiet = half * modes
    ups = reflect.shape[0]
    pairs_total = pairs * n
    rough = cells.shape[1]
    share = rough // n
    piece = quiet // 4
    batch = min(16, modes)
    per_dir = modes // batch
    order = [d for d in range(1, dirs, 2)] + [d for d in range(0, dirs, 2)]
    chunks = [(d, b) for d in order for b in range(per_dir)]

    fetched = copies((
        (cells_in, cells), (weight_in, weight), (dir_cos_in, dir_cos), (velocity_in, velocity),
        (rate_in, rate), (spectrum_in, spectrum), (dir_cos_in, dir_row),
        (velocity_in, velocity_row), (rate_in, rate_row), (spectrum_in, spectrum_row),
        (weight_in, weight_row), (heat_in, heat), (reflect_in, reflect),
    ), psem)
    for copy in fetched:
        copy.start()

    def load(i):
        d, b = chunks[i]
        where = pl.ds(d * modes + b * batch, batch)
        return [
            pltpu.make_async_copy(
                x.at[where, :, pl.ds(k * LANE, LANE)], xv.at[where, k], lsem.at[k, i]
            )
            for k in range(strips)
        ]

    for i in range(len(chunks)):
        for copy in load(i):
            copy.start()

    barrier = pltpu.get_barrier_semaphore()
    for off in range(1, n):
        pl.semaphore_signal(
            barrier, inc=1, device_id={"mode": lax.rem(me + off, n)}, device_id_type=MESH
        )

    @pl.when(sp > 0)
    def _():
        pl.semaphore_signal(barrier, inc=1, device_id={"space": sp - 1}, device_id_type=MESH)

    @pl.when(sp < ns - 1)
    def _():
        pl.semaphore_signal(barrier, inc=1, device_id={"space": sp + 1}, device_id_type=MESH)

    @pl.when(sp == 0)
    def _():
        lo[...] = jnp.zeros_like(lo)

    @pl.when(sp == ns - 1)
    def _():
        hi[...] = jnp.zeros_like(hi)

    acc[...] = jnp.zeros_like(acc)
    acc2[...] = jnp.zeros_like(acc2)
    for copy in fetched:
        copy.wait()
    marks[...] = jnp.where(iota((width, rough), 0) == lax.rem(cells[...], width), 1.0, 0.0).astype(
        BF16
    )
    on_row[...] = jnp.where(iota((rows, rough), 0) == cells[...] // width, 1.0, 0.0)
    def down_copy(i):
        d, b = chunks[i]
        where = pl.ds(d * modes + b * batch, batch)
        return send(
            first.at[where], hi.at[where], hsem.at[0, i], hsem.at[1, i], "space",
            lax.rem(sp + ns - 1, ns),
        )

    def up_copy(i):
        d, b = chunks[i]
        where = pl.ds(d * modes + b * batch, batch)
        return send(
            last.at[where], lo.at[where], hsem.at[2, i], hsem.at[3, i], "space",
            lax.rem(sp + 1, ns),
        )

    def halo_wait(i):
        @pl.when(sp > 0)
        def _():
            down_copy(i).wait_send()
            up_copy(i).wait_recv()

        @pl.when(sp < ns - 1)
        def _():
            up_copy(i).wait_send()
            down_copy(i).wait_recv()

    def add_up(i):
        d, b = chunks[i]
        base = d * modes + b * batch
        for copy in load(i):
            copy.wait()
        w = weight[0, me * dirs + d]

        def add_rows(r, carry):
            here = pl.ds(pl.multiple_of(r * SUB, SUB), SUB)
            for k in range(strips):
                value = xv[base, k, here, :]
                for t in range(1, batch):
                    value = value + xv[base + t, k, here, :]
                acc[here, pl.ds(k * LANE, LANE)] += w * value
            return carry

        lax.fori_loop(0, total_rows // SUB, add_rows, 0)

    def share_edges(i):
        d, b = chunks[i]
        base = d * modes + b * batch

        def edges(t, carry):
            p = base + t
            for z in range(planes):
                for k in range(strips):
                    cols = pl.ds(k * LANE, LANE)
                    first[p, pl.ds(z, 1), cols] = xv[p, k, pl.ds(z * rows, 1), :]
                    last[p, pl.ds(z, 1), cols] = xv[p, k, pl.ds((z + 1) * rows - 1, 1), :]
            return carry

        lax.fori_loop(0, batch, edges, 0)

        @pl.when(sp > 0)
        def _():
            down_copy(i).start()

        @pl.when(sp < ns - 1)
        def _():
            up_copy(i).start()

    row, lane = iota((SUB, LANE), 0), iota((SUB, LANE), 1)
    places = tiles(rows, width)
    last_row, last_col = rows - SUB, width - LANE

    def gain(d, kind, m):
        return jnp.broadcast_to(table[d, kind, pl.ds(m, 1), :], (SUB, LANE))

    def cosines(d):
        return [jnp.abs(dir_cos[axis, me * dirs + d]) for axis in range(3)]

    def tabulate():
        same = iota((modes, modes), 0) == iota((modes, modes), 1)

        def column(values):
            return jnp.sum(jnp.where(same, values, 0.0), axis=1, keepdims=True)

        v, e, f = column(velocity_row[...]), column(rate_row[...]), column(spectrum_row[...])
        for d in range(dirs):
            inv = 1.0 / (1.0 + e + v * cosines(d)[2])
            for kind, value in enumerate((inv, inv * v, inv * (e * f))):
                table[d, kind] = jnp.broadcast_to(value, (modes, LANE))

    halo_done = set()

    def sweep(d, start, stop):
        for i, (dd, b) in enumerate(chunks):
            if dd == d and b * batch < stop and start < (b + 1) * batch and i not in halo_done:
                halo_done.add(i)
                halo_wait(i)
        s = me * dirs + d
        w = weight[0, s]
        low_x, low_y = splat(dir_cos[0, s]) >= 0.0, splat(dir_cos[1, s]) >= 0.0
        cx, cy, cz = cosines(d)
        shift_x = jnp.where(dir_cos[0, s] >= 0.0, 1, SUB - 1)
        step_x = jnp.where(dir_cos[0, s] >= 0.0, -1, 1)
        shift_y = jnp.where(dir_cos[1, s] >= 0.0, 1, LANE - 1)
        head_x, tail_x = low_x & (row == 0), ~low_x & (row == SUB - 1)
        head_y, tail_y = low_y & (lane == 0), ~low_y & (lane == LANE - 1)
        wide = 2

        def some(g, carry):
            sets, before = [], []
            for t in range(wide):
                m = start + g * wide + t
                inv, fast = gain(d, 0, m), gain(d, 1, m)
                kx, ky = fast * cx, fast * cy
                sets.append((
                    d * modes + m, inv - kx - ky, kx, fast * cz,
                    ky, jnp.where(head_y, 0.0, ky), jnp.where(tail_y, 0.0, ky),
                ))
                if d % 2 == 0:
                    before.append({
                        (r, c): smooth[pl.ds(r, SUB), pl.ds(c, LANE)]
                        * xv[(d + 1) * modes + m, c // LANE, pl.ds(r, SUB), :]
                        for r, c in places
                    })
                else:
                    before.append(None)
            for z in range(planes) if d % 2 == 0 else reversed(range(planes)):
                sums = {}
                for t in range(wide):
                    p, k0, kx, kp, ky, ky_head, ky_tail = sets[t]
                    own = {
                        (r, c): xv[p, c // LANE, pl.ds(z * rows + r, SUB), :] for r, c in places
                    }
                    along = {at: pltpu.roll(own[at], shift_y, 1) for at in places}
                    now, ones = {}, {}
                    for r, c in places:
                        k, at_row = c // LANE, z * rows + r
                        under = over = None
                        if r == 0:
                            under = jnp.broadcast_to(
                                lo[p, pl.ds(z, 1), pl.ds(c, LANE)], (SUB, LANE)
                            )
                        if r == last_row:
                            over = jnp.broadcast_to(
                                hi[p, pl.ds(z, 1), pl.ds(c, LANE)], (SUB, LANE)
                            )
                        if 0 < at_row < total_rows - SUB:
                            one = xv[p, k, pl.ds(at_row + step_x, SUB), :]
                        else:
                            one = pltpu.roll(own[r, c], shift_x, 0)
                            if under is None:
                                under = pltpu.roll(own[r - SUB, c], 1, 0)
                            if over is None:
                                over = pltpu.roll(own[r + SUB, c], SUB - 1, 0)
                        if under is not None:
                            one = jnp.where(head_x, under, one)
                        if over is not None:
                            one = jnp.where(tail_x, over, one)
                        ones[r, c] = one
                    for r, c in places:
                        cols = pl.ds(c, LANE)
                        one = ones[r, c]
                        two = along[r, c]
                        if c > 0:
                            two = jnp.where(head_y, along[r, c - LANE], two)
                        if c < last_col:
                            two = jnp.where(tail_y, along[r, c + LANE], two)
                        weigh = ky
                        if c == 0:
                            weigh = ky_head
                        if c == last_col:
                            weigh = ky_tail if c else jnp.where(tail_y, 0.0, ky_head)
                        value = k0 * own[r, c] + kx * one + weigh * two
                        if before[t] is not None:
                            value = value + kp * before[t][r, c]
                        now[r, c] = value
                        xv[p, c // LANE, pl.ds(z * rows + r, SUB), :] = value
                        sums[r, c] = sums[r, c] + value if t else value
                    before[t] = now
                for r, c in places:
                    acc2[pl.ds(z * rows + r, SUB), pl.ds(c, LANE)] += w * sums[r, c]
            return carry

        lax.fori_loop(0, (stop - start) // wide, some, 0)

    def settle(h, start, stop):
        wide = 2
        up, down = 2 * h, 2 * h + 1

        def some(g, carry):
            sets, values = [], []
            for t in range(wide):
                m = start + g * wide + t
                sets.append((m, gain(up, 1, m) * cosines(up)[2], gain(up, 2, m)))
                values.append({
                    (r, c): heat[pl.ds(r, SUB), pl.ds(c, LANE)] * spectrum[0, m] for r, c in places
                })
            for d, z in [(down, z) for z in reversed(range(planes))] + [
                (up, z) for z in range(planes)
            ]:
                for r, c in places:
                    here, cols = pl.ds(z * rows + r, SUB), pl.ds(c, LANE)
                    level = equil[here, cols]
                    for t in range(wide):
                        m, kp, ks = sets[t]
                        value = values[t][r, c]
                        if d == up and z == 0:
                            value = value * smooth[pl.ds(r, SUB), cols]
                        value = kp * value + ks * level
                        values[t][r, c] = value
                        xv[d * modes + m, c // LANE, here, :] += value
            return carry

        lax.fori_loop(0, (stop - start) // wide, some, 0)

    def pair_of(q):
        return (2 * (q // modes) + 1) * modes + q % modes

    def at_slots(values):
        k = values.shape[0]
        high, low = split(values.reshape(k * rows, width))
        column = marks[...]
        got = dot(high, column) + dot(low, column)
        return jnp.sum(got.reshape(k, rows, rough) * on_row[...][None], axis=1)

    def shares(values):
        return [values[:, i * share : (i + 1) * share] for i in range(n)]

    def outward(part, off):
        target = lax.rem(me + off, n)
        here = pl.ds(part * piece, piece)
        return send(
            outbox.at[target, here], inbox.at[me, here], gone.at[part, off], come.at[part, off],
            "mode", target,
        )

    def arrival(part, off):
        source = lax.rem(me + n - off, n)
        here = pl.ds(part * piece, piece)
        return send(
            outbox.at[source, here], inbox.at[source, here], gone.at[part, off],
            come.at[part, off], "mode", source,
        )

    def homeward(off):
        target = lax.rem(me + off, n)
        mine = pl.ds(pl.multiple_of(target * quiet, quiet), quiet)
        return [
            send(
                picked.at[mine], returned.at[me], back_gone.at[0, off], back_come.at[0, off],
                "mode", target,
            ),
            send(shine, glow.at[me], back_gone.at[1, off], back_come.at[1, off], "mode", target),
        ]

    def return_of(off):
        source = lax.rem(me + n - off, n)
        mine = pl.ds(pl.multiple_of(me * quiet, quiet), quiet)
        return [
            send(
                picked.at[mine], returned.at[source], back_gone.at[0, off], back_come.at[0, off],
                "mode", source,
            ),
            send(
                shine, glow.at[source], back_gone.at[1, off], back_come.at[1, off], "mode", source
            ),
        ]

    def launch(part):
        q = part * piece
        sweep(2 * (q // modes) + 1, q % modes, q % modes + piece)
        strip = [xv[pl.ds(pair_of(q), piece), k, pl.ds(0, rows), :] for k in range(strips)]
        got = at_slots(jnp.concatenate(strip, axis=2))
        for i, value in enumerate(shares(got)):
            outbox[i, pl.ds(q, piece), :] = value
        for off in range(1, n):
            outward(part, off).start()
        inbox[me, pl.ds(q, piece), :] = outbox[me, pl.ds(q, piece), :]

    def own_share(values):
        total = jnp.zeros((values.shape[0], share), values.dtype)
        for i, value in enumerate(shares(values)):
            total = jnp.where(me == i, value, total)
        return total

    def choose():
        for part in range(4):
            for off in range(1, n):
                arrival(part, off).wait_recv()
        lanes = response.shape[1]
        levels = at_slots(equil[...].reshape(planes, rows, width))
        face = at_slots(heat[...].reshape(1, rows, width))
        spare = jnp.zeros((lanes - planes - 1, rough), F32)
        sources = own_share(jnp.concatenate([levels, face, spare], axis=0))
        lift = fine_dot(response[...], sources)
        inbox[...] += lift.reshape(n, quiet, share)
        wanted[...] = own_share(reflect[...])

        def one(k, carry):
            want = wanted[pl.ds(k, 1), :]
            value = None
            for j in range(ups):
                source = inbox[j // half, pl.ds((j % half) * modes, modes), :]
                value = source if j == 0 else jnp.where(want == j, source, value)
            picked[pl.ds(pl.multiple_of(k * modes, modes), modes), :] = value
            return carry

        lax.fori_loop(0, ups, one, 0)
        shine[...] = fine_dot(gains[...], picked[...])
        for off in range(1, n):
            for copy in homeward(off):
                copy.start()
        returned[me] = picked[pl.ds(pl.multiple_of(me * quiet, quiet), quiet), :]
        glow[me] = shine[...]

    def prepare():
        size, lanes = ups * modes, response.shape[1]
        which = iota((size, 1), 0)
        modal = iota((size, modes), 1) == lax.rem(which, modes)
        angle = iota((size, 2 * ups), 1) == 2 * (which // modes) + 1

        def spread(mask, values):
            return jnp.sum(jnp.where(mask, values, 0.0), axis=1, keepdims=True)

        v, e = spread(modal, velocity_row[...]), spread(modal, rate_row[...])
        f = spread(modal, spectrum_row[...])
        turn = v * spread(angle, jnp.abs(dir_row[pl.ds(2, 1), :]))
        inv = 1.0 / (1.0 + e + turn)
        kp, power = turn * inv, inv * (e * f)
        at = iota((size, lanes), 1)
        out = jnp.zeros((size, lanes), F32)
        for z in range(planes):
            out = jnp.where(at == z, power, out)
            power = power * kp
        power = f * kp
        for z in range(planes - 1):
            power = power * kp
        response[...] = jnp.where(at == planes, power, out)

        which = iota((1, size), 1)

        def along(values, index):
            length = values.shape[1]
            same = iota((length, length), 0) == iota((length, length), 1)
            column = jnp.sum(jnp.where(same, values, 0.0), axis=1, keepdims=True)
            mask = iota((length, size), 0) == index
            return jnp.sum(jnp.where(mask, column, 0.0), axis=0, keepdims=True)

        modal, angle = lax.rem(which, modes), 2 * (which // modes)
        v, e = along(velocity_row[...], modal), along(rate_row[...], modal)
        turn = v * along(jnp.abs(dir_row[pl.ds(2, 1), :]), angle)
        kp = turn / (1.0 + e + turn)
        power = 0.9 * along(weight_row[...], angle)
        for z in range(planes):
            power = power * kp
            gains[pl.ds(z, 1), :] = power

    def find_rough():
        live[...] = jnp.where(iota((rows, rough), 1) < count[0], on_row[...], 0.0)
        rough_at = lax.dot_general(
            live[...].astype(BF16), marks[...], (((1,), (1,)), ((), ())), preferred_element_type=F32
        )
        smooth[...] = jnp.where(rough_at > 0.5, 0.0, 0.9)

    opening = Reduction(acc, slots1, part1, equil, sems1, n)
    closing = Reduction(acc2, slots2, part2, summed, sems2, n)

    tabulate()
    add_up(0)
    low = jnp.where(sp > 0, 1, 0)
    high = jnp.where(sp < ns - 1, 1, 0)
    pl.semaphore_wait(barrier, n - 1 + low + high)
    share_edges(0)
    for i in range(1, len(chunks)):
        add_up(i)
        share_edges(i)
    opening.start()
    for part in range(4):
        launch(part)
        if part == 2:
            opening.combine(lambda value: squash(value * (1.0 / pairs_total)))
    find_rough()
    slices = [(h, m) for h in range(half) for m in range(0, modes, SUB)]
    middle = len(slices) // 2
    for h, m in slices[:middle]:
        sweep(2 * h, m, m + SUB)
    prepare()
    opening.finish()
    choose()
    for h, m in slices[middle:]:
        sweep(2 * h, m, m + SUB)
    closing.start()
    for i, (h, m) in enumerate(slices):
        settle(h, m, m + SUB)
    closing.combine(lambda value: value)
    for off in range(1, n):
        for copy in return_of(off):
            copy.wait_recv()
    for off in range(1, n):
        for part in range(4):
            outward(part, off).wait_send()
        for copy in homeward(off):
            copy.wait_send()
    closing.finish()


def main_step(scalars, count, heat, cells, reflect, x, n, ns, planes):
    pairs, total_rows, width = x.shape
    rows = total_rows // planes
    modes = scalars[1].shape[1]
    quiet = pairs // 2
    rough = cells.shape[1]
    every = reflect.shape[0] * modes
    share = rough // n
    n_chunks = (pairs // modes) * (modes // min(16, modes))
    flat = (total_rows, width)
    part = (total_rows // n, width)
    halo = pltpu.VMEM((pairs, planes, width), F32)
    lanes = -(-(planes + 1) // 16) * 16
    return pl.pallas_call(
        functools.partial(main_kernel, n, ns, planes),
        out_shape=(
            jax.ShapeDtypeStruct((pairs, width // LANE, total_rows, LANE), F32),
            jax.ShapeDtypeStruct((n, quiet, share), F32),
            jax.ShapeDtypeStruct((n, planes, share), F32),
            jax.ShapeDtypeStruct(flat, F32),
            jax.ShapeDtypeStruct(flat, F32),
            jax.ShapeDtypeStruct((rows, width), F32),
            jax.ShapeDtypeStruct((rows, rough), F32),
            jax.ShapeDtypeStruct((width, rough), BF16),
        ),
        in_specs=[whole(pltpu.SMEM)] + [whole(pltpu.HBM)] * 9,
        out_specs=(whole(),) * 8,
        scratch_shapes=[
            *(pltpu.SMEM(a.shape, a.dtype) for a in scalars),
            *(pltpu.VMEM(a.shape, a.dtype) for a in (*scalars, heat, cells, reflect)),
            halo, halo, halo, halo,
            pltpu.VMEM(flat, F32),
            pltpu.VMEM((n, *part), F32),
            pltpu.VMEM(part, F32),
            pltpu.VMEM(flat, F32),
            pltpu.VMEM((n, *part), F32),
            pltpu.VMEM(part, F32),
            pltpu.VMEM((pairs // modes, 3, modes, LANE), F32),
            pltpu.VMEM((n, quiet, share), F32),
            pltpu.VMEM((n, quiet, share), F32),
            pltpu.VMEM((reflect.shape[0], share), jnp.int32),
            pltpu.VMEM((every, share), F32),
            pltpu.VMEM((planes, share), F32),
            pltpu.VMEM((rows, rough), F32),
            pltpu.VMEM((every, lanes), F32),
            pltpu.VMEM((planes, every), F32),
            pltpu.SemaphoreType.DMA((13,)),
            pltpu.SemaphoreType.DMA((width // LANE, n_chunks)),
            pltpu.SemaphoreType.DMA((4, n_chunks)),
            pltpu.SemaphoreType.DMA((4, n)),
            pltpu.SemaphoreType.DMA((4, n)),
            pltpu.SemaphoreType.DMA((4, n)),
            pltpu.SemaphoreType.DMA((4, n)),
            pltpu.SemaphoreType.DMA((2, n)),
            pltpu.SemaphoreType.DMA((2, n)),
        ],
        compiler_params=pltpu.CompilerParams(
            collective_id=0, has_side_effects=True, vmem_limit_bytes=28 * MIB
        ),
        name="main_step",
    )(count, *in_hbm(*scalars, heat, cells, reflect, x))


def emit_kernel(
    planes, pairs_total, dir_cos_in, velocity_in, rate_in, spectrum_in, weight_in, heat_in,
    xv, returned, glow, equil, summed, smooth, live, marks,
    out, energy,
    dir_cos, velocity, rate, dir_row, velocity_row, rate_row, spectrum_row, weight_row, heat,
    rising, inflow, moments, psem, sem,
):
    pairs, strips, total_rows, _ = xv.shape
    width = strips * LANE
    rows = total_rows // planes
    modes = velocity.shape[1]
    dirs = pairs // modes
    half = dirs // 2
    rough = live.shape[1]
    n = returned.shape[0]
    every = n * half * modes
    batch = min(8, modes)
    me = lax.axis_index("mode")
    places = tiles(rows, width)

    def whole_dir(d):
        where = pl.ds(d * modes, modes)
        return [
            pltpu.make_async_copy(
                xv.at[where, k], out.at[where, :, pl.ds(k * LANE, LANE)], sem.at[d, k]
            )
            for k in range(strips)
        ]

    def piece(d, b):
        return pltpu.make_async_copy(
            rising.at[pl.ds(d // 2 * modes + b * batch, batch)],
            out.at[pl.ds(d * modes + b * batch, batch)], sem.at[d, b],
        )

    fetched = copies((
        (dir_cos_in, dir_cos), (velocity_in, velocity), (rate_in, rate), (dir_cos_in, dir_row),
        (velocity_in, velocity_row), (rate_in, rate_row), (spectrum_in, spectrum_row),
        (weight_in, weight_row), (heat_in, heat),
    ), psem)
    for copy in fetched:
        copy.start()
    for d in range(1, dirs, 2):
        for copy in whole_dir(d):
            copy.start()
    for copy in fetched:
        copy.wait()

    group = min(16, modes)
    for d in range(0, dirs, 2):
        cz = jnp.abs(dir_cos[2, me * dirs + d])
        for g in range(modes // group):
            first = pl.ds(d // 2 * modes + g * group, group)
            own = jnp.concatenate([returned[i, first, :] for i in range(n)], axis=1)
            spread = own[:, None, :] * live[...][None]
            put = turned_dot(spread.reshape(group * rows, rough), marks[...])
            inflow[...] = 0.9 * put.reshape(group, rows, width)
            for b in range(g * group // batch, (g + 1) * group // batch):
                def one(i, carry):
                    m = b * batch + i
                    turn = velocity[0, m] * cz
                    ratio = splat(turn) / splat(1.0 + rate[0, m] + turn)
                    for r, c in places:
                        cols = pl.ds(c, LANE)
                        value = inflow[m - g * group, pl.ds(r, SUB), cols]
                        for z in range(planes):
                            here = pl.ds(z * rows + r, SUB)
                            value = ratio * value
                            rising[d // 2 * modes + m, here, cols] = (
                                xv[d * modes + m, c // LANE, here, :] + value
                            )
                    return carry

                lax.fori_loop(0, batch, one, 0)
                piece(d, b).start()

    n_dirs = weight_row.shape[1]

    def column(values):
        size = values.shape[1]
        same = iota((size, size), 0) == iota((size, size), 1)
        return jnp.sum(jnp.where(same, values, 0.0), axis=1, keepdims=True)

    which = iota((1, every), 1)

    def spread_over(values, index):
        size = values.shape[1]
        mask = iota((size, every), 0) == index
        return jnp.sum(jnp.where(mask, column(values), 0.0), axis=0, keepdims=True)

    modal, angle = lax.rem(which, modes), 2 * (which // modes)
    v, e = spread_over(velocity_row[...], modal), spread_over(rate_row[...], modal)
    f = spread_over(spectrum_row[...], modal)
    turn = v * spread_over(jnp.abs(dir_row[pl.ds(2, 1), :]), angle)
    w_up, w_down = spread_over(weight_row[...], angle), spread_over(weight_row[...], angle + 1)
    inv = 1.0 / (1.0 + e + turn)
    kp, ks = turn * inv, inv * (e * f)
    top = 2 * planes + 2
    power = jnp.ones_like(kp)
    for q in range(top):
        for i, scale in enumerate((w_up * ks, w_down * ks, w_up * f, w_down * f)):
            total = jnp.sum(scale * power, axis=1, keepdims=True)
            moments[i, pl.ds(q, 1), :] = jnp.broadcast_to(total, (1, LANE))
        power = power * kp
    at_slot = jnp.concatenate([glow[i] for i in range(n)], axis=1)
    spread = at_slot[:, None, :] * live[...][None]
    rough_part = turned_dot(spread.reshape(total_rows, rough), marks[...])

    def moment(i, q):
        return jnp.broadcast_to(moments[i, pl.ds(q, 1), :], (SUB, LANE))

    for r, c in places:
        cols = pl.ds(c, LANE)
        levels = [equil[pl.ds(z * rows + r, SUB), cols] for z in range(planes)]
        face = heat[pl.ds(r, SUB), cols]
        plain = smooth[pl.ds(r, SUB), cols]
        for z in range(planes):
            here = pl.ds(z * rows + r, SUB)
            value = summed[here, cols] + rough_part[z * rows + r : z * rows + r + SUB, c : c + LANE]
            value = value + moment(3, planes - z) * face
            turned = moment(2, z + 1 + planes) * face
            for y in range(planes):
                if y <= z:
                    value = value + moment(0, z - y) * levels[y]
                if y >= z:
                    value = value + moment(1, y - z) * levels[y]
                turned = turned + moment(0, z + 1 + y) * levels[y]
            energy[here, cols] = (value + plain * turned) * (1.0 / pairs_total)
    for d in range(dirs):
        if d % 2:
            for copy in whole_dir(d):
                copy.wait()
        else:
            for b in range(modes // batch):
                piece(d, b).wait()


def emit_step(planes, pairs_total, scalars, heat, parts):
    xv = parts[0]
    pairs, strips, total_rows, _ = xv.shape
    width = strips * LANE
    modes = scalars[1].shape[1]
    rows = total_rows // planes
    return pl.pallas_call(
        functools.partial(emit_kernel, planes, pairs_total),
        out_shape=(
            jax.ShapeDtypeStruct((pairs, total_rows, width), F32),
            jax.ShapeDtypeStruct((total_rows, width), F32),
        ),
        in_specs=[whole(pltpu.HBM)] * 6 + [whole()] * len(parts),
        out_specs=(whole(pltpu.HBM), whole()),
        scratch_shapes=[
            *(pltpu.SMEM(a.shape, a.dtype) for a in scalars[:3]),
            *(pltpu.VMEM(a.shape, a.dtype) for a in (*scalars, heat)),
            pltpu.VMEM((pairs // 2, total_rows, width), F32),
            pltpu.VMEM((min(16, modes), rows, width), F32),
            pltpu.VMEM((4, -(-(2 * planes + 2) // SUB) * SUB, LANE), F32),
            pltpu.SemaphoreType.DMA((9,)),
            pltpu.SemaphoreType.DMA((pairs // modes, max(strips, modes // min(8, modes)))),
        ],
        compiler_params=pltpu.CompilerParams(vmem_limit_bytes=28 * MIB),
        name="emit_step",
    )(*in_hbm(*scalars, heat), *parts)


def per_device(
    n, ns, intensity, dir_cos, velocity, rate, spectrum, weight, heat, rough_cells, rough_count,
    rough_map,
):
    pairs, planes, rows, width = intensity.shape
    x = intensity.reshape(pairs, planes * rows, width)
    scalars = (dir_cos, velocity[None], rate[None], spectrum[None], weight[None])
    parts = main_step(scalars, rough_count, heat, rough_cells[None], rough_map.T, x, n, ns, planes)
    fresh, energy = emit_step(planes, pairs * n, scalars, heat, parts)
    return fresh.reshape(intensity.shape), energy.reshape(planes, rows, width)


def solution(mesh):
    n, ns = mesh.shape["mode"], mesh.shape["space"]
    in_specs = (
        P("mode", None, "space", None),
        P(),
        P(),
        P(),
        P(),
        P(),
        P("space", None),
        P("space"),
        P("space"),
        P("space", None),
    )
    out_specs = (P("mode", None, "space", None), P(None, "space", None))
    return jax.shard_map(
        functools.partial(per_device, n, ns),
        mesh=mesh,
        in_specs=in_specs,
        out_specs=out_specs,
        check_vma=False,
    )
```

```python
import functools

import jax
import jax.numpy as jnp
from jax import lax
from jax.experimental import pallas as pl
from jax.experimental.pallas import tpu as pltpu
from jax.sharding import PartitionSpec as P

MESH = pl.DeviceIdType.MESH
F32 = jnp.float32
BF16 = jnp.bfloat16
SUB, LANE = 8, 128
MIB = 1 << 20


def whole(space=pltpu.VMEM):
    return pl.BlockSpec(memory_space=space)


def in_hbm(*arrays):
    return tuple(pltpu.with_memory_space_constraint(a, pltpu.HBM) for a in arrays)


def squash(energy):
    return energy / (1.0 + 0.3 * jnp.abs(energy))


def send(src, dst, ssem, rsem, axis, target):
    return pltpu.make_async_remote_copy(
        src_ref=src,
        dst_ref=dst,
        send_sem=ssem,
        recv_sem=rsem,
        device_id={axis: target},
        device_id_type=MESH,
    )


class Reduction:
    def __init__(self, acc, slots, part, total, sems, n):
        self.acc, self.slots, self.part, self.total = acc, slots, part, total
        self.sems, self.n = sems, n
        self.me = lax.axis_index("mode")
        self.rows = acc.shape[0] // n

    def chunk(self, i):
        return pl.ds(pl.multiple_of(i * self.rows, self.rows), self.rows)

    def outward(self, off):
        target = lax.rem(self.me + off, self.n)
        return send(
            self.acc.at[self.chunk(target)], self.slots.at[off],
            self.sems.at[0, off], self.sems.at[1, off], "mode", target,
        )

    def spread(self, off):
        target = lax.rem(self.me + off, self.n)
        return send(
            self.part, self.total.at[self.chunk(self.me)],
            self.sems.at[2, off], self.sems.at[3, off], "mode", target,
        )

    def start(self):
        for off in range(1, self.n):
            self.outward(off).start()

    def combine(self, finish):
        for off in range(1, self.n):
            self.outward(off).wait_recv()
        value = self.acc[self.chunk(self.me), :]
        for off in range(1, self.n):
            value = value + self.slots[off]
        self.part[...] = finish(value)
        for off in range(1, self.n):
            self.spread(off).start()
        self.total[self.chunk(self.me), :] = self.part[...]

    def finish(self):
        for off in range(1, self.n):
            source = lax.rem(self.me + self.n - off, self.n)
            send(
                self.part, self.total.at[self.chunk(source)],
                self.sems.at[2, off], self.sems.at[3, off], "mode", source,
            ).wait_recv()
        for off in range(1, self.n):
            self.outward(off).wait_send()
            self.spread(off).wait_send()


def split(value):
    high = value.astype(BF16)
    return high, (value - high.astype(F32)).astype(BF16)


def splat(value):
    return jnp.full((SUB, LANE), value, F32)


def tiles(rows, width):
    return [(r, c) for r in range(0, rows, SUB) for c in range(0, width, LANE)]


def dot(a, b):
    return jnp.dot(a, b, preferred_element_type=F32)


def fine_dot(a, b):
    a_high, a_low = split(a)
    b_high, b_low = split(b)
    return dot(a_high, b_high) + (dot(a_high, b_low) + dot(a_low, b_high))


def turned_dot(a, b):
    contract = (((1,), (1,)), ((), ()))
    high, low = split(a)
    return lax.dot_general(high, b, contract, preferred_element_type=F32) + lax.dot_general(
        low, b, contract, preferred_element_type=F32
    )


def iota(shape, axis):
    return lax.broadcasted_iota(jnp.int32, shape, axis)


def copies(pairs, sem):
    return [pltpu.make_async_copy(src, dst, sem.at[i]) for i, (src, dst) in enumerate(pairs)]


def main_kernel(
    n, ns, planes,
    count, dir_cos_in, velocity_in, rate_in, spectrum_in, weight_in, heat_in, cells_in, reflect_in,
    x,
    xv, returned, glow, equil, summed, smooth, live, marks,
    dir_cos, velocity, rate, spectrum, weight, dir_row, velocity_row, rate_row, spectrum_row,
    weight_row, heat, cells, reflect,
    lo, hi, first, last, acc, slots1, part1, acc2, slots2, part2,
    table, outbox, inbox, wanted, picked, shine, on_row, response, gains,
    psem, lsem, hsem, sems1, sems2, gone, come, back_gone, back_come,
):
    me, sp = lax.axis_index("mode"), lax.axis_index("space")
    pairs, strips, total_rows, _ = xv.shape
    width = strips * LANE
    rows = total_rows // planes
    modes = velocity.shape[1]
    dirs = pairs // modes
    half = dirs // 2
    quiet = half * modes
    ups = reflect.shape[0]
    pairs_total = pairs * n
    rough = cells.shape[1]
    share = rough // n
    piece = quiet // 4
    batch = min(16, modes)
    per_dir = modes // batch
    order = [d for d in range(1, dirs, 2)] + [d for d in range(0, dirs, 2)]
    chunks = [(d, b) for d in order for b in range(per_dir)]

    fetched = copies((
        (cells_in, cells), (weight_in, weight), (dir_cos_in, dir_cos), (velocity_in, velocity),
        (rate_in, rate), (spectrum_in, spectrum), (dir_cos_in, dir_row),
        (velocity_in, velocity_row), (rate_in, rate_row), (spectrum_in, spectrum_row),
        (weight_in, weight_row), (heat_in, heat), (reflect_in, reflect),
    ), psem)
    for copy in fetched:
        copy.start()

    def load(i):
        d, b = chunks[i]
        where = pl.ds(d * modes + b * batch, batch)
        return [
            pltpu.make_async_copy(
                x.at[where, :, pl.ds(k * LANE, LANE)], xv.at[where, k], lsem.at[k, i]
            )
            for k in range(strips)
        ]

    for i in range(len(chunks)):
        for copy in load(i):
            copy.start()

    barrier = pltpu.get_barrier_semaphore()
    for off in range(1, n):
        pl.semaphore_signal(
            barrier, inc=1, device_id={"mode": lax.rem(me + off, n)}, device_id_type=MESH
        )

    @pl.when(sp > 0)
    def _():
        pl.semaphore_signal(barrier, inc=1, device_id={"space": sp - 1}, device_id_type=MESH)

    @pl.when(sp < ns - 1)
    def _():
        pl.semaphore_signal(barrier, inc=1, device_id={"space": sp + 1}, device_id_type=MESH)

    @pl.when(sp == 0)
    def _():
        lo[...] = jnp.zeros_like(lo)

    @pl.when(sp == ns - 1)
    def _():
        hi[...] = jnp.zeros_like(hi)

    acc[...] = jnp.zeros_like(acc)
    acc2[...] = jnp.zeros_like(acc2)
    for copy in fetched:
        copy.wait()
    marks[...] = jnp.where(iota((width, rough), 0) == lax.rem(cells[...], width), 1.0, 0.0).astype(
        BF16
    )
    on_row[...] = jnp.where(iota((rows, rough), 0) == cells[...] // width, 1.0, 0.0)
    def down_copy(i):
        d, b = chunks[i]
        where = pl.ds(d * modes + b * batch, batch)
        return send(
            first.at[where], hi.at[where], hsem.at[0, i], hsem.at[1, i], "space",
            lax.rem(sp + ns - 1, ns),
        )

    def up_copy(i):
        d, b = chunks[i]
        where = pl.ds(d * modes + b * batch, batch)
        return send(
            last.at[where], lo.at[where], hsem.at[2, i], hsem.at[3, i], "space",
            lax.rem(sp + 1, ns),
        )

    def halo_wait(i):
        @pl.when(sp > 0)
        def _():
            down_copy(i).wait_send()
            up_copy(i).wait_recv()

        @pl.when(sp < ns - 1)
        def _():
            up_copy(i).wait_send()
            down_copy(i).wait_recv()

    def add_up(i):
        d, b = chunks[i]
        base = d * modes + b * batch
        for copy in load(i):
            copy.wait()
        w = weight[0, me * dirs + d]

        def add_rows(r, carry):
            here = pl.ds(pl.multiple_of(r * SUB, SUB), SUB)
            for k in range(strips):
                value = xv[base, k, here, :]
                for t in range(1, batch):
                    value = value + xv[base + t, k, here, :]
                acc[here, pl.ds(k * LANE, LANE)] += w * value
            return carry

        lax.fori_loop(0, total_rows // SUB, add_rows, 0)

    def share_edges(i):
        d, b = chunks[i]
        base = d * modes + b * batch

        def edges(t, carry):
            p = base + t
            for z in range(planes):
                for k in range(strips):
                    cols = pl.ds(k * LANE, LANE)
                    first[p, pl.ds(z, 1), cols] = xv[p, k, pl.ds(z * rows, 1), :]
                    last[p, pl.ds(z, 1), cols] = xv[p, k, pl.ds((z + 1) * rows - 1, 1), :]
            return carry

        lax.fori_loop(0, batch, edges, 0)

        @pl.when(sp > 0)
        def _():
            down_copy(i).start()

        @pl.when(sp < ns - 1)
        def _():
            up_copy(i).start()

    row, lane = iota((SUB, LANE), 0), iota((SUB, LANE), 1)
    places = tiles(rows, width)
    last_row, last_col = rows - SUB, width - LANE

    def gain(d, kind, m):
        return jnp.broadcast_to(table[d, kind, pl.ds(m, 1), :], (SUB, LANE))

    def cosines(d):
        return [jnp.abs(dir_cos[axis, me * dirs + d]) for axis in range(3)]

    def tabulate():
        same = iota((modes, modes), 0) == iota((modes, modes), 1)

        def column(values):
            return jnp.sum(jnp.where(same, values, 0.0), axis=1, keepdims=True)

        v, e, f = column(velocity_row[...]), column(rate_row[...]), column(spectrum_row[...])
        for d in range(dirs):
            inv = 1.0 / (1.0 + e + v * cosines(d)[2])
            for kind, value in enumerate((inv, inv * v, inv * (e * f))):
                table[d, kind] = jnp.broadcast_to(value, (modes, LANE))

    halo_done = set()

    def sweep(d, start, stop):
        for i, (dd, b) in enumerate(chunks):
            if dd == d and b * batch < stop and start < (b + 1) * batch and i not in halo_done:
                halo_done.add(i)
                halo_wait(i)
        s = me * dirs + d
        w = weight[0, s]
        low_x, low_y = splat(dir_cos[0, s]) >= 0.0, splat(dir_cos[1, s]) >= 0.0
        cx, cy, cz = cosines(d)
        shift_x = jnp.where(dir_cos[0, s] >= 0.0, 1, SUB - 1)
        shift_y = jnp.where(dir_cos[1, s] >= 0.0, 1, LANE - 1)
        head_x, tail_x = low_x & (row == 0), ~low_x & (row == SUB - 1)
        head_y, tail_y = low_y & (lane == 0), ~low_y & (lane == LANE - 1)
        wide = 4

        def some(g, carry):
            sets, before = [], []
            for t in range(wide):
                m = start + g * wide + t
                inv, fast = gain(d, 0, m), gain(d, 1, m)
                kx, ky = fast * cx, fast * cy
                sets.append((
                    d * modes + m, inv - kx - ky, kx, fast * cz,
                    ky, jnp.where(head_y, 0.0, ky), jnp.where(tail_y, 0.0, ky),
                ))
                if d % 2 == 0:
                    before.append({
                        (r, c): smooth[pl.ds(r, SUB), pl.ds(c, LANE)]
                        * xv[(d + 1) * modes + m, c // LANE, pl.ds(r, SUB), :]
                        for r, c in places
                    })
                else:
                    before.append(None)
            for z in range(planes) if d % 2 == 0 else reversed(range(planes)):
                sums = {}
                for t in range(wide):
                    p, k0, kx, kp, ky, ky_head, ky_tail = sets[t]
                    own = {
                        (r, c): xv[p, c // LANE, pl.ds(z * rows + r, SUB), :] for r, c in places
                    }
                    along = {at: pltpu.roll(own[at], shift_y, 1) for at in places}
                    side = {at: pltpu.roll(own[at], shift_x, 0) for at in places}
                    now, ones = {}, {}
                    for r, c in places:
                        if r == 0:
                            under = jnp.broadcast_to(
                                lo[p, pl.ds(z, 1), pl.ds(c, LANE)], (SUB, LANE)
                            )
                        else:
                            under = side[r - SUB, c]
                        if r == last_row:
                            over = jnp.broadcast_to(
                                hi[p, pl.ds(z, 1), pl.ds(c, LANE)], (SUB, LANE)
                            )
                        else:
                            over = side[r + SUB, c]
                        ones[r, c] = jnp.where(head_x, under, jnp.where(tail_x, over, side[r, c]))
                    for r, c in places:
                        cols = pl.ds(c, LANE)
                        one = ones[r, c]
                        two = along[r, c]
                        if c > 0:
                            two = jnp.where(head_y, along[r, c - LANE], two)
                        if c < last_col:
                            two = jnp.where(tail_y, along[r, c + LANE], two)
                        weigh = ky
                        if c == 0:
                            weigh = ky_head
                        if c == last_col:
                            weigh = ky_tail if c else jnp.where(tail_y, 0.0, ky_head)
                        value = k0 * own[r, c] + kx * one + weigh * two
                        if before[t] is not None:
                            value = value + kp * before[t][r, c]
                        now[r, c] = value
                        xv[p, c // LANE, pl.ds(z * rows + r, SUB), :] = value
                        sums[r, c] = sums[r, c] + value if t else value
                    before[t] = now
                for r, c in places:
                    acc2[pl.ds(z * rows + r, SUB), pl.ds(c, LANE)] += w * sums[r, c]
            return carry

        lax.fori_loop(0, (stop - start) // wide, some, 0)

    def settle(h, start, stop):
        wide = 2
        up, down = 2 * h, 2 * h + 1

        def some(g, carry):
            sets, values = [], []
            for t in range(wide):
                m = start + g * wide + t
                sets.append((m, gain(up, 1, m) * cosines(up)[2], gain(up, 2, m)))
                values.append({
                    (r, c): heat[pl.ds(r, SUB), pl.ds(c, LANE)] * spectrum[0, m] for r, c in places
                })
            for d, z in [(down, z) for z in reversed(range(planes))] + [
                (up, z) for z in range(planes)
            ]:
                for r, c in places:
                    here, cols = pl.ds(z * rows + r, SUB), pl.ds(c, LANE)
                    level = equil[here, cols]
                    for t in range(wide):
                        m, kp, ks = sets[t]
                        value = values[t][r, c]
                        if d == up and z == 0:
                            value = value * smooth[pl.ds(r, SUB), cols]
                        value = kp * value + ks * level
                        values[t][r, c] = value
                        xv[d * modes + m, c // LANE, here, :] += value
            return carry

        lax.fori_loop(0, (stop - start) // wide, some, 0)

    def pair_of(q):
        return (2 * (q // modes) + 1) * modes + q % modes

    def at_slots(values):
        k = values.shape[0]
        high, low = split(values.reshape(k * rows, width))
        column = marks[...]
        got = dot(high, column) + dot(low, column)
        return jnp.sum(got.reshape(k, rows, rough) * on_row[...][None], axis=1)

    def shares(values):
        return [values[:, i * share : (i + 1) * share] for i in range(n)]

    def outward(part, off):
        target = lax.rem(me + off, n)
        here = pl.ds(part * piece, piece)
        return send(
            outbox.at[target, here], inbox.at[me, here], gone.at[part, off], come.at[part, off],
            "mode", target,
        )

    def arrival(part, off):
        source = lax.rem(me + n - off, n)
        here = pl.ds(part * piece, piece)
        return send(
            outbox.at[source, here], inbox.at[source, here], gone.at[part, off],
            come.at[part, off], "mode", source,
        )

    def homeward(off):
        target = lax.rem(me + off, n)
        mine = pl.ds(pl.multiple_of(target * quiet, quiet), quiet)
        return [
            send(
                picked.at[mine], returned.at[me], back_gone.at[0, off], back_come.at[0, off],
                "mode", target,
            ),
            send(shine, glow.at[me], back_gone.at[1, off], back_come.at[1, off], "mode", target),
        ]

    def return_of(off):
        source = lax.rem(me + n - off, n)
        mine = pl.ds(pl.multiple_of(me * quiet, quiet), quiet)
        return [
            send(
                picked.at[mine], returned.at[source], back_gone.at[0, off], back_come.at[0, off],
                "mode", source,
            ),
            send(
                shine, glow.at[source], back_gone.at[1, off], back_come.at[1, off], "mode", source
            ),
        ]

    def launch(part):
        q = part * piece
        sweep(2 * (q // modes) + 1, q % modes, q % modes + piece)
        strip = [xv[pl.ds(pair_of(q), piece), k, pl.ds(0, rows), :] for k in range(strips)]
        got = at_slots(jnp.concatenate(strip, axis=2))
        for i, value in enumerate(shares(got)):
            outbox[i, pl.ds(q, piece), :] = value
        for off in range(1, n):
            outward(part, off).start()
        inbox[me, pl.ds(q, piece), :] = outbox[me, pl.ds(q, piece), :]

    def own_share(values):
        total = jnp.zeros((values.shape[0], share), values.dtype)
        for i, value in enumerate(shares(values)):
            total = jnp.where(me == i, value, total)
        return total

    def choose():
        for part in range(4):
            for off in range(1, n):
                arrival(part, off).wait_recv()
        lanes = response.shape[1]
        levels = at_slots(equil[...].reshape(planes, rows, width))
        face = at_slots(heat[...].reshape(1, rows, width))
        spare = jnp.zeros((lanes - planes - 1, rough), F32)
        sources = own_share(jnp.concatenate([levels, face, spare], axis=0))
        lift = fine_dot(response[...], sources)
        inbox[...] += lift.reshape(n, quiet, share)
        wanted[...] = own_share(reflect[...])

        def one(k, carry):
            want = wanted[pl.ds(k, 1), :]
            value = None
            for j in range(ups):
                source = inbox[j // half, pl.ds((j % half) * modes, modes), :]
                value = source if j == 0 else jnp.where(want == j, source, value)
            picked[pl.ds(pl.multiple_of(k * modes, modes), modes), :] = value
            return carry

        lax.fori_loop(0, ups, one, 0)
        shine[...] = fine_dot(gains[...], picked[...])
        for off in range(1, n):
            for copy in homeward(off):
                copy.start()
        returned[me] = picked[pl.ds(pl.multiple_of(me * quiet, quiet), quiet), :]
        glow[me] = shine[...]

    def prepare():
        size, lanes = ups * modes, response.shape[1]
        which = iota((size, 1), 0)
        modal = iota((size, modes), 1) == lax.rem(which, modes)
        angle = iota((size, 2 * ups), 1) == 2 * (which // modes) + 1

        def spread(mask, values):
            return jnp.sum(jnp.where(mask, values, 0.0), axis=1, keepdims=True)

        v, e = spread(modal, velocity_row[...]), spread(modal, rate_row[...])
        f = spread(modal, spectrum_row[...])
        turn = v * spread(angle, jnp.abs(dir_row[pl.ds(2, 1), :]))
        inv = 1.0 / (1.0 + e + turn)
        kp, power = turn * inv, inv * (e * f)
        at = iota((size, lanes), 1)
        out = jnp.zeros((size, lanes), F32)
        for z in range(planes):
            out = jnp.where(at == z, power, out)
            power = power * kp
        power = f * kp
        for z in range(planes - 1):
            power = power * kp
        response[...] = jnp.where(at == planes, power, out)

        which = iota((1, size), 1)

        def along(values, index):
            length = values.shape[1]
            same = iota((length, length), 0) == iota((length, length), 1)
            column = jnp.sum(jnp.where(same, values, 0.0), axis=1, keepdims=True)
            mask = iota((length, size), 0) == index
            return jnp.sum(jnp.where(mask, column, 0.0), axis=0, keepdims=True)

        modal, angle = lax.rem(which, modes), 2 * (which // modes)
        v, e = along(velocity_row[...], modal), along(rate_row[...], modal)
        turn = v * along(jnp.abs(dir_row[pl.ds(2, 1), :]), angle)
        kp = turn / (1.0 + e + turn)
        power = 0.9 * along(weight_row[...], angle)
        for z in range(planes):
            power = power * kp
            gains[pl.ds(z, 1), :] = power

    def find_rough():
        live[...] = jnp.where(iota((rows, rough), 1) < count[0], on_row[...], 0.0)
        rough_at = lax.dot_general(
            live[...].astype(BF16), marks[...], (((1,), (1,)), ((), ())), preferred_element_type=F32
        )
        smooth[...] = jnp.where(rough_at > 0.5, 0.0, 0.9)

    opening = Reduction(acc, slots1, part1, equil, sems1, n)
    closing = Reduction(acc2, slots2, part2, summed, sems2, n)

    tabulate()
    find_rough()
    add_up(0)
    low = jnp.where(sp > 0, 1, 0)
    high = jnp.where(sp < ns - 1, 1, 0)
    pl.semaphore_wait(barrier, n - 1 + low + high)
    share_edges(0)
    prepare()
    for i in range(1, len(chunks)):
        add_up(i)
        share_edges(i)
    opening.start()
    for part in range(4):
        launch(part)
        if part == 2:
            opening.combine(lambda value: squash(value * (1.0 / pairs_total)))
    slices = [(h, m) for h in range(half) for m in range(0, modes, SUB)]
    for h, m in slices:
        sweep(2 * h, m, m + SUB)
    closing.start()
    opening.finish()
    choose()
    for i, (h, m) in enumerate(slices):
        settle(h, m, m + SUB)
    closing.combine(lambda value: value)
    for off in range(1, n):
        for copy in return_of(off):
            copy.wait_recv()
    for off in range(1, n):
        for part in range(4):
            outward(part, off).wait_send()
        for copy in homeward(off):
            copy.wait_send()
    closing.finish()


def main_step(scalars, count, heat, cells, reflect, x, n, ns, planes):
    pairs, total_rows, width = x.shape
    rows = total_rows // planes
    modes = scalars[1].shape[1]
    quiet = pairs // 2
    rough = cells.shape[1]
    every = reflect.shape[0] * modes
    share = rough // n
    n_chunks = (pairs // modes) * (modes // min(16, modes))
    flat = (total_rows, width)
    part = (total_rows // n, width)
    halo = pltpu.VMEM((pairs, planes, width), F32)
    lanes = -(-(planes + 1) // 16) * 16
    return pl.pallas_call(
        functools.partial(main_kernel, n, ns, planes),
        out_shape=(
            jax.ShapeDtypeStruct((pairs, width // LANE, total_rows, LANE), F32),
            jax.ShapeDtypeStruct((n, quiet, share), F32),
            jax.ShapeDtypeStruct((n, planes, share), F32),
            jax.ShapeDtypeStruct(flat, F32),
            jax.ShapeDtypeStruct(flat, F32),
            jax.ShapeDtypeStruct((rows, width), F32),
            jax.ShapeDtypeStruct((rows, rough), F32),
            jax.ShapeDtypeStruct((width, rough), BF16),
        ),
        in_specs=[whole(pltpu.SMEM)] + [whole(pltpu.HBM)] * 9,
        out_specs=(whole(),) * 8,
        scratch_shapes=[
            *(pltpu.SMEM(a.shape, a.dtype) for a in scalars),
            *(pltpu.VMEM(a.shape, a.dtype) for a in (*scalars, heat, cells, reflect)),
            halo, halo, halo, halo,
            pltpu.VMEM(flat, F32),
            pltpu.VMEM((n, *part), F32),
            pltpu.VMEM(part, F32),
            pltpu.VMEM(flat, F32),
            pltpu.VMEM((n, *part), F32),
            pltpu.VMEM(part, F32),
            pltpu.VMEM((pairs // modes, 3, modes, LANE), F32),
            pltpu.VMEM((n, quiet, share), F32),
            pltpu.VMEM((n, quiet, share), F32),
            pltpu.VMEM((reflect.shape[0], share), jnp.int32),
            pltpu.VMEM((every, share), F32),
            pltpu.VMEM((planes, share), F32),
            pltpu.VMEM((rows, rough), F32),
            pltpu.VMEM((every, lanes), F32),
            pltpu.VMEM((planes, every), F32),
            pltpu.SemaphoreType.DMA((13,)),
            pltpu.SemaphoreType.DMA((width // LANE, n_chunks)),
            pltpu.SemaphoreType.DMA((4, n_chunks)),
            pltpu.SemaphoreType.DMA((4, n)),
            pltpu.SemaphoreType.DMA((4, n)),
            pltpu.SemaphoreType.DMA((4, n)),
            pltpu.SemaphoreType.DMA((4, n)),
            pltpu.SemaphoreType.DMA((2, n)),
            pltpu.SemaphoreType.DMA((2, n)),
        ],
        compiler_params=pltpu.CompilerParams(
            collective_id=0, has_side_effects=True, vmem_limit_bytes=28 * MIB
        ),
        name="main_step",
    )(count, *in_hbm(*scalars, heat, cells, reflect, x))


def emit_kernel(
    planes, pairs_total, dir_cos_in, velocity_in, rate_in, spectrum_in, weight_in, heat_in,
    xv, returned, glow, equil, summed, smooth, live, marks,
    out, energy,
    dir_cos, velocity, rate, dir_row, velocity_row, rate_row, spectrum_row, weight_row, heat,
    rising, inflow, moments, psem, sem,
):
    pairs, strips, total_rows, _ = xv.shape
    width = strips * LANE
    rows = total_rows // planes
    modes = velocity.shape[1]
    dirs = pairs // modes
    half = dirs // 2
    rough = live.shape[1]
    n = returned.shape[0]
    every = n * half * modes
    batch = min(8, modes)
    me = lax.axis_index("mode")
    places = tiles(rows, width)

    def whole_dir(d):
        where = pl.ds(d * modes, modes)
        return [
            pltpu.make_async_copy(
                xv.at[where, k], out.at[where, :, pl.ds(k * LANE, LANE)], sem.at[d, k]
            )
            for k in range(strips)
        ]

    def piece(d, b):
        return pltpu.make_async_copy(
            rising.at[pl.ds(d // 2 * modes + b * batch, batch)],
            out.at[pl.ds(d * modes + b * batch, batch)], sem.at[d, b],
        )

    fetched = copies((
        (dir_cos_in, dir_cos), (velocity_in, velocity), (rate_in, rate), (dir_cos_in, dir_row),
        (velocity_in, velocity_row), (rate_in, rate_row), (spectrum_in, spectrum_row),
        (weight_in, weight_row), (heat_in, heat),
    ), psem)
    for copy in fetched:
        copy.start()
    for d in range(1, dirs, 2):
        for copy in whole_dir(d):
            copy.start()
    for copy in fetched:
        copy.wait()

    group = min(16, modes)
    for d in range(0, dirs, 2):
        cz = jnp.abs(dir_cos[2, me * dirs + d])
        for g in range(modes // group):
            first = pl.ds(d // 2 * modes + g * group, group)
            own = jnp.concatenate([returned[i, first, :] for i in range(n)], axis=1)
            spread = own[:, None, :] * live[...][None]
            put = turned_dot(spread.reshape(group * rows, rough), marks[...])
            inflow[...] = 0.9 * put.reshape(group, rows, width)
            for b in range(g * group // batch, (g + 1) * group // batch):
                def one(i, carry):
                    m = b * batch + i
                    turn = velocity[0, m] * cz
                    ratio = splat(turn) / splat(1.0 + rate[0, m] + turn)
                    for r, c in places:
                        cols = pl.ds(c, LANE)
                        value = inflow[m - g * group, pl.ds(r, SUB), cols]
                        for z in range(planes):
                            here = pl.ds(z * rows + r, SUB)
                            value = ratio * value
                            rising[d // 2 * modes + m, here, cols] = (
                                xv[d * modes + m, c // LANE, here, :] + value
                            )
                    return carry

                lax.fori_loop(0, batch, one, 0)
                piece(d, b).start()

    n_dirs = weight_row.shape[1]

    def column(values):
        size = values.shape[1]
        same = iota((size, size), 0) == iota((size, size), 1)
        return jnp.sum(jnp.where(same, values, 0.0), axis=1, keepdims=True)

    which = iota((1, every), 1)

    def spread_over(values, index):
        size = values.shape[1]
        mask = iota((size, every), 0) == index
        return jnp.sum(jnp.where(mask, column(values), 0.0), axis=0, keepdims=True)

    modal, angle = lax.rem(which, modes), 2 * (which // modes)
    v, e = spread_over(velocity_row[...], modal), spread_over(rate_row[...], modal)
    f = spread_over(spectrum_row[...], modal)
    turn = v * spread_over(jnp.abs(dir_row[pl.ds(2, 1), :]), angle)
    w_up, w_down = spread_over(weight_row[...], angle), spread_over(weight_row[...], angle + 1)
    inv = 1.0 / (1.0 + e + turn)
    kp, ks = turn * inv, inv * (e * f)
    top = 2 * planes + 2
    power = jnp.ones_like(kp)
    for q in range(top):
        for i, scale in enumerate((w_up * ks, w_down * ks, w_up * f, w_down * f)):
            total = jnp.sum(scale * power, axis=1, keepdims=True)
            moments[i, pl.ds(q, 1), :] = jnp.broadcast_to(total, (1, LANE))
        power = power * kp
    at_slot = jnp.concatenate([glow[i] for i in range(n)], axis=1)
    spread = at_slot[:, None, :] * live[...][None]
    rough_part = turned_dot(spread.reshape(total_rows, rough), marks[...])

    def moment(i, q):
        return jnp.broadcast_to(moments[i, pl.ds(q, 1), :], (SUB, LANE))

    for r, c in places:
        cols = pl.ds(c, LANE)
        levels = [equil[pl.ds(z * rows + r, SUB), cols] for z in range(planes)]
        face = heat[pl.ds(r, SUB), cols]
        plain = smooth[pl.ds(r, SUB), cols]
        for z in range(planes):
            here = pl.ds(z * rows + r, SUB)
            value = summed[here, cols] + rough_part[z * rows + r : z * rows + r + SUB, c : c + LANE]
            value = value + moment(3, planes - z) * face
            turned = moment(2, z + 1 + planes) * face
            for y in range(planes):
                if y <= z:
                    value = value + moment(0, z - y) * levels[y]
                if y >= z:
                    value = value + moment(1, y - z) * levels[y]
                turned = turned + moment(0, z + 1 + y) * levels[y]
            energy[here, cols] = (value + plain * turned) * (1.0 / pairs_total)
    for d in range(dirs):
        if d % 2:
            for copy in whole_dir(d):
                copy.wait()
        else:
            for b in range(modes // batch):
                piece(d, b).wait()


def emit_step(planes, pairs_total, scalars, heat, parts):
    xv = parts[0]
    pairs, strips, total_rows, _ = xv.shape
    width = strips * LANE
    modes = scalars[1].shape[1]
    rows = total_rows // planes
    return pl.pallas_call(
        functools.partial(emit_kernel, planes, pairs_total),
        out_shape=(
            jax.ShapeDtypeStruct((pairs, total_rows, width), F32),
            jax.ShapeDtypeStruct((total_rows, width), F32),
        ),
        in_specs=[whole(pltpu.HBM)] * 6 + [whole()] * len(parts),
        out_specs=(whole(pltpu.HBM), whole()),
        scratch_shapes=[
            *(pltpu.SMEM(a.shape, a.dtype) for a in scalars[:3]),
            *(pltpu.VMEM(a.shape, a.dtype) for a in (*scalars, heat)),
            pltpu.VMEM((pairs // 2, total_rows, width), F32),
            pltpu.VMEM((min(16, modes), rows, width), F32),
            pltpu.VMEM((4, -(-(2 * planes + 2) // SUB) * SUB, LANE), F32),
            pltpu.SemaphoreType.DMA((9,)),
            pltpu.SemaphoreType.DMA((pairs // modes, max(strips, modes // min(8, modes)))),
        ],
        compiler_params=pltpu.CompilerParams(vmem_limit_bytes=28 * MIB),
        name="emit_step",
    )(*in_hbm(*scalars, heat), *parts)


def per_device(
    n, ns, intensity, dir_cos, velocity, rate, spectrum, weight, heat, rough_cells, rough_count,
    rough_map,
):
    pairs, planes, rows, width = intensity.shape
    x = intensity.reshape(pairs, planes * rows, width)
    scalars = (dir_cos, velocity[None], rate[None], spectrum[None], weight[None])
    parts = main_step(scalars, rough_count, heat, rough_cells[None], rough_map.T, x, n, ns, planes)
    fresh, energy = emit_step(planes, pairs * n, scalars, heat, parts)
    return fresh.reshape(intensity.shape), energy.reshape(planes, rows, width)


def solution(mesh):
    n, ns = mesh.shape["mode"], mesh.shape["space"]
    in_specs = (
        P("mode", None, "space", None),
        P(),
        P(),
        P(),
        P(),
        P(),
        P("space", None),
        P("space"),
        P("space"),
        P("space", None),
    )
    out_specs = (P("mode", None, "space", None), P(None, "space", None))
    return jax.shard_map(
        functools.partial(per_device, n, ns),
        mesh=mesh,
        in_specs=in_specs,
        out_specs=out_specs,
        check_vma=False,
    )
```
